512 devices in a mesh: mem: 64 (over y, x, core), head: 8 (over z).
Axes of the slice: x: 4, y: 8, z: 8, core: 2. Of those that a mesh axis runs over, the one named last changes fastest.
Arguments:
- queries: bfloat16 [16384, 4096], P(('mem', 'head')), may hold values from -512 to 512
- local_keys: bfloat16 [16384, 1024], P(('mem', 'head')), may hold values from -6 to 6
- local_values: bfloat16 [16384, 1024], P(('mem', 'head')), may hold values from -12 to 12
- memory_keys: bfloat16 [262144, 1024], P('mem', 'head'), may hold values from -6 to 6
- memory_values: bfloat16 [262144, 1024], P('mem', 'head'), may hold values from -12 to 12
- block_ids: int32 [128, 8, 32], P('mem', 'head'), may hold values from 0 to 2047, as said below
- mixing_offset_per_head: float32 [32], P('head'), may hold values from -2 to 2
Outputs:
- attended: bfloat16 [16384, 4096], P(('mem', 'head'))
The draws below stay inside these ranges and needn't reach their ends.
Inputs may be any that keep to these rules, and one draw needn't show every extreme that they name: Each row block_ids[b, h] names 32 different blocks. Over the 2 query blocks of one index of mem and one key-value head, the named blocks with one value of n // 32 are at most 1 different ones; for some value exactly 1, each named by all 2 of those query blocks.
All inputs are finite; a program needn't handle non-finite values.
Results may differ from the reference program's by a relative error of at most 0.0033.
Values may be sent and summed in bfloat16 or wider, within the bound.
No kernel may reach another device: no remote copies, remote signals or barrier semaphores. Data moves between devices by JAX's collectives and lax.ppermute only.
A program may use at most 64 MiB of HBM per device.

```python
import math
import jax
import jax.numpy as jnp
from jax import lax

H = 32
KVH = 8
HD = 128
QB = 128
BL = 128
TOPK = 32
WINDOW = 256
SHARD_SPAN = 256
MB_DEV = 32
TOKENS = 16384
MBLOCKS = 2048
MENTRIES = 262144
N_MEM = 64


def drawn_field(key, row_count, column_count, spread):
    field = jax.random.normal(jax.random.fold_in(key, 3), (row_count, column_count), jnp.float32)
    return jnp.clip(field, -6.0, 6.0) * spread


def drawn_keys(own_key, row_count):
    field = drawn_field(own_key, row_count, KVH * HD, 1.0)
    return field


def draw_local_keys(key, part):
    return drawn_keys(jax.random.fold_in(key, 21), TOKENS).astype(jnp.bfloat16)


def draw_memory_keys(key, part):
    return drawn_keys(jax.random.fold_in(key, 31), MENTRIES).astype(jnp.bfloat16)


def draw_queries(key, part):
    field = drawn_field(jax.random.fold_in(key, 41), TOKENS, H * HD, 2.0)
    return field.astype(jnp.bfloat16)


def draw_block_ids(key, part):
    block_rows = SHARD_SPAN // QB
    per_owner = (2 * TOPK + N_MEM - 1) // N_MEM
    width_all = N_MEM * per_owner
    pick_scores = jax.random.randint(jax.random.fold_in(key, 1), (N_MEM, KVH, N_MEM, MB_DEV), 0, 1 << 16)
    pick_scores = pick_scores * MB_DEV + jnp.arange(MB_DEV, dtype=jnp.int32)
    unused, picked = lax.top_k(pick_scores, per_owner)
    owners = jnp.arange(N_MEM, dtype=jnp.int32)
    candidates = (owners[:, None] * MB_DEV + picked).reshape(N_MEM, KVH, width_all)
    proposed_holder = jnp.repeat(owners, per_owner)
    heaviest_segment = jax.random.randint(jax.random.fold_in(key, 2), (KVH,), 0, N_MEM)
    center = jax.random.randint(jax.random.fold_in(key, 3), (N_MEM, KVH), 0, N_MEM)
    spacing_distance = jnp.abs(proposed_holder[None, None, :] - center[:, :, None])
    spacing_distance = jnp.minimum(spacing_distance, N_MEM - spacing_distance)
    closeness_measure = (N_MEM - spacing_distance) * 64 // N_MEM
    small_disturbance = jax.random.randint(jax.random.fold_in(key, 4), (N_MEM, block_rows, KVH, width_all), 0, 64)
    measure_addition = jnp.where(proposed_holder[None, :] == heaviest_segment[:, None], 1 << 12, 0)
    measure_grid_array = small_disturbance + closeness_measure[:, None, :, :] + measure_addition[None, None, :, :]
    measure_grid_array = measure_grid_array * width_all + jnp.arange(width_all, dtype=jnp.int32)
    unused_top, chosen = lax.top_k(measure_grid_array, TOPK)
    spread_cand = jnp.broadcast_to(candidates[:, None, :, :], (N_MEM, block_rows, KVH, width_all))
    chosen_ids = jnp.take_along_axis(spread_cand, chosen, axis=3)
    return chosen_ids.reshape(N_MEM * block_rows, KVH, TOPK).astype(jnp.int32)


def steps_of(key, extent, shards, least, largest):
    def one(axis_at, shards_of):
        steps = jax.random.uniform(jax.random.fold_in(jax.random.fold_in(key, 6), axis_at), (shards_of,), jnp.float32, least / len(shards), largest / len(shards))
        return jnp.repeat(jnp.exp(steps), extent[axis_at] // shards_of).reshape((-1,) + (1,) * (len(extent) - axis_at - 1))

    loudness = one(*shards[0])
    for cut in shards[1:]:
        loudness = loudness * one(*cut)
    return loudness


def centred(rng, extent, deviation, bound, shards=(), held_as=jnp.bfloat16):
    values = deviation * jax.random.normal(rng, extent, jnp.float32)
    if shards:
        values = values * steps_of(rng, extent, shards, -0.22, 0.18)
    return jnp.clip(values, -bound, bound).astype(held_as)


def setup_inputs(seed: int = 0) -> dict:
    splits = jax.random.split(jax.random.key(seed), 8)
    queries = draw_queries(jax.random.fold_in(splits[7], 71), 0)
    local_keys = draw_local_keys(jax.random.fold_in(splits[7], 71), 0)
    local_values = centred(splits[2], (TOKENS, KVH * HD), 2.0, 12.0, ((0, 512),))
    memory_keys = draw_memory_keys(jax.random.fold_in(splits[7], 71), 0)
    memory_values = centred(splits[4], (MENTRIES, KVH * HD), 2.0, 12.0, ((0, 64), (1, 8)))
    block_ids = draw_block_ids(jax.random.fold_in(splits[7], 71), 0)
    mixing_offset_per_head = jnp.clip(jax.random.uniform(splits[6], (H,), jnp.float32, -2.0, 2.0) * steps_of(splits[6], (H,), ((0, 8),), -0.4, 0.0), -2.0, 2.0)
    return {"queries": queries, "local_keys": local_keys, "local_values": local_values, "memory_keys": memory_keys, "memory_values": memory_values, "block_ids": block_ids, "mixing_offset_per_head": mixing_offset_per_head}


def attend_block(query_block, key_rows, value_rows, allowed):
    score_scale = 1.0 / math.sqrt(query_block.shape[-1])
    measure_grid_array = jnp.einsum('tgd,kd->tgk', query_block.astype(jnp.float32), key_rows.astype(jnp.float32), precision=lax.Precision.HIGHEST) * score_scale
    if allowed is not None:
        measure_grid_array = jnp.where(allowed[:, None, :], measure_grid_array, -1e+30)
    highest = lax.optimization_barrier(jnp.max(measure_grid_array, axis=2, keepdims=True))
    weights = jnp.exp(measure_grid_array - highest)
    denominator = lax.optimization_barrier(jnp.sum(weights, axis=2, keepdims=True))
    rounded = lax.optimization_barrier(weights.astype(jnp.bfloat16)).astype(jnp.float32)
    mixed = jnp.einsum('tgk,kd->tgd', rounded, value_rows.astype(jnp.float32), precision=lax.Precision.HIGHEST)
    return mixed / denominator

def reference(queries, local_keys, local_values, memory_keys, memory_values, block_ids, mixing_offset_per_head):
    group_size = H // KVH
    segment_count = TOKENS // QB
    span = WINDOW + QB
    query_grid = queries.reshape(segment_count, QB, KVH, group_size, HD)
    front = jnp.zeros((WINDOW, KVH * HD), local_keys.dtype)
    padded_keys = jnp.concatenate([front, local_keys], axis=0)
    padded_values = jnp.concatenate([front, local_values], axis=0)
    key_store = memory_keys.reshape(MBLOCKS, BL, KVH, HD)
    value_store = memory_values.reshape(MBLOCKS, BL, KVH, HD)
    gate_share = jax.nn.sigmoid(mixing_offset_per_head).reshape(KVH, group_size)

    def one_pair(couple_ordinal):
        block_index = (couple_ordinal // KVH).astype(jnp.int32)
        head_index = (couple_ordinal % KVH).astype(jnp.int32)
        zero = jnp.zeros((), jnp.int32)
        query_block = lax.dynamic_slice(query_grid, (block_index, zero, head_index, zero, zero), (1, QB, 1, group_size, HD)).reshape(QB, group_size, HD)
        start = (block_index * QB).astype(jnp.int32)
        key_rows = lax.dynamic_slice(padded_keys, (start, (head_index * HD).astype(jnp.int32)), (span, HD))
        value_rows = lax.dynamic_slice(padded_values, (start, (head_index * HD).astype(jnp.int32)), (span, HD))
        query_pos = start + jnp.arange(QB, dtype=jnp.int32)
        key_pos = start - WINDOW + jnp.arange(span, dtype=jnp.int32)
        spacing_distance = query_pos[:, None] - key_pos[None, :]
        allowed = (key_pos[None, :] >= 0) & (spacing_distance >= 0) & (spacing_distance < WINDOW)
        local_part = attend_block(query_block, key_rows, value_rows, allowed)
        chosen = block_ids[block_index, head_index]
        memory_key_rows = key_store[chosen, :, head_index, :].reshape(TOPK * BL, HD)
        memory_value_rows = value_store[chosen, :, head_index, :].reshape(TOPK * BL, HD)
        memory_part = attend_block(query_block, memory_key_rows, memory_value_rows, None)
        share = gate_share[head_index][None, :, None]
        return (share * memory_part + (1.0 - share) * local_part).astype(jnp.bfloat16)
    blended = lax.map(one_pair, jnp.arange(segment_count * KVH, dtype=jnp.int32))
    grid = blended.reshape(segment_count, KVH, QB, group_size, HD)
    return jnp.transpose(grid, (0, 2, 1, 3, 4)).reshape(TOKENS, H * HD)
```

```python
import functools
import math

import jax
import jax.numpy as jnp
from jax import lax
from jax.experimental import pallas as pl
from jax.experimental.pallas import tpu as pltpu
from jax.sharding import PartitionSpec as P

HD = 128
QB = 128
BL = 128
TOPK = 32
WINDOW = 256
GROUP = 4
SCALE = 1.0 / math.sqrt(HD)


def gather_kernel(blocks, idx_ref, src_ref, out_ref, sem):
    def start(i, carry):
        pltpu.make_async_copy(src_ref.at[idx_ref[i]], out_ref.at[i], sem).start()
        return carry

    lax.fori_loop(0, blocks, start, 0)
    pltpu.make_async_copy(out_ref, out_ref, sem).wait()


def gather_blocks(idx, src):
    blocks = idx.shape[0]
    return pl.pallas_call(
        functools.partial(gather_kernel, blocks),
        out_shape=jax.ShapeDtypeStruct((blocks,) + src.shape[1:], src.dtype),
        grid_spec=pltpu.PrefetchScalarGridSpec(
            num_scalar_prefetch=1,
            grid=(1,),
            in_specs=[pl.BlockSpec(memory_space=pl.ANY)],
            out_specs=pl.BlockSpec(memory_space=pl.ANY),
            scratch_shapes=[pltpu.SemaphoreType.DMA],
        ),
        name="gather_blocks",
    )(idx, src)


def score_kernel(
    owner_ref, place_ref, gate_ref, qkv_ref, before_ref, keys_ref,
    probs_ref, total_ref, local_ref,
    q_scr, k_scr, v_scr, s_scr,
):
    block = pl.program_id(0)
    mem_index, head_index = place_ref[0], place_ref[1]

    @pl.when(block == 0)
    def _():
        for i in range(8):
            at = lax.rem(head_index + 8 - i, 8)
            rows = pl.ds(i * 32, 32)
            for g in range(GROUP):
                q_scr[g, rows, :] = qkv_ref[at, :, pl.ds(g * HD, HD)]
            k_scr[pl.ds(WINDOW + i * 32, 32), :] = qkv_ref[at, :, pl.ds(4 * HD, HD)]
            v_scr[pl.ds(WINDOW + i * 32, 32), :] = qkv_ref[at, :, pl.ds(5 * HD, HD)]
            k_scr[pl.ds(i * 32, 32), :] = before_ref[at, :, pl.ds(0, HD)]
            v_scr[pl.ds(i * 32, 32), :] = before_ref[at, :, pl.ds(HD, HD)]

    start = pl.multiple_of(block * QB, QB)
    q = q_scr[:, pl.ds(start, QB), :].reshape(GROUP * QB, HD)

    span = WINDOW + QB
    lk = k_scr[pl.ds(start, span), :]
    lv = v_scr[pl.ds(start, span), :]
    ls = lax.dot_general(q, lk, (((1,), (1,)), ((), ())), preferred_element_type=jnp.float32) * SCALE
    t = lax.broadcasted_iota(jnp.int32, (QB, span), 0)
    s = lax.broadcasted_iota(jnp.int32, (QB, span), 1)
    apart = t + WINDOW - s
    known = mem_index * (2 * QB) + block * QB - WINDOW + s >= 0
    allowed = known & (apart >= 0) & (apart < WINDOW)
    ls = jnp.where(allowed[None], ls.reshape(GROUP, QB, span), -1e30).reshape(GROUP * QB, span)
    lm = jnp.max(ls, axis=1, keepdims=True)
    lw = jnp.exp(ls - lm)
    lt = jnp.sum(lw, axis=1, keepdims=True)
    lo = jnp.dot(lw.astype(jnp.bfloat16), lv, preferred_element_type=jnp.float32) / lt
    for g in range(GROUP):
        rows = pl.ds(g * QB, QB)
        local_ref[0, rows, :] = lo[g * QB : (g + 1) * QB] * (1.0 - gate_ref[g])

    def score(j, high):
        sc = lax.dot_general(
            q, keys_ref[owner_ref[block * TOPK + j]], (((1,), (1,)), ((), ())),
            preferred_element_type=jnp.float32,
        ) * SCALE
        s_scr[j] = sc
        return jnp.maximum(high, sc)

    high = lax.fori_loop(0, TOPK, score, jnp.full((GROUP * QB, BL), -jnp.inf, jnp.float32))
    high = jnp.broadcast_to(jnp.max(high, axis=1, keepdims=True), (GROUP * QB, BL))

    def weigh(j, total):
        w = jnp.exp(s_scr[j] - high)
        probs_ref[0, j] = w.astype(jnp.bfloat16)
        return total + w

    total = lax.fori_loop(0, TOPK, weigh, jnp.zeros((GROUP * QB, BL), jnp.float32))
    total = jnp.broadcast_to(jnp.sum(total, axis=1, keepdims=True), (GROUP * QB, BL))
    for g in range(GROUP):
        rows = pl.ds(g * QB, QB)
        total_ref[0, rows, :] = gate_ref[g] / total[g * QB : (g + 1) * QB]


def scores(owner, place, gate, qkv, before, keys):
    whole = lambda shape: pl.BlockSpec(shape, lambda b, *_: (0,) * len(shape))
    rows = GROUP * QB
    return pl.pallas_call(
        score_kernel,
        out_shape=(
            jax.ShapeDtypeStruct((2, TOPK, rows, BL), jnp.bfloat16),
            jax.ShapeDtypeStruct((2, rows, HD), jnp.float32),
            jax.ShapeDtypeStruct((2, rows, HD), jnp.float32),
        ),
        grid_spec=pltpu.PrefetchScalarGridSpec(
            num_scalar_prefetch=3,
            grid=(2,),
            in_specs=[whole(qkv.shape), whole(before.shape), whole(keys.shape)],
            out_specs=(
                pl.BlockSpec((1, TOPK, rows, BL), lambda b, *_: (b, 0, 0, 0)),
                pl.BlockSpec((1, rows, HD), lambda b, *_: (b, 0, 0)),
                pl.BlockSpec((1, rows, HD), lambda b, *_: (b, 0, 0)),
            ),
            scratch_shapes=[
                pltpu.VMEM((GROUP, 2 * QB, HD), jnp.bfloat16),
                pltpu.VMEM((WINDOW + 2 * QB, HD), jnp.bfloat16),
                pltpu.VMEM((WINDOW + 2 * QB, HD), jnp.bfloat16),
                pltpu.VMEM((TOPK, rows, BL), jnp.float32),
            ],
        ),
        name="scores",
    )(owner, place, gate, qkv, before, keys)


CHUNK = 8


def mix_kernel(owner_ref, probs_ref, values_ref, total_ref, local_ref, out_ref, acc):
    block, part = pl.program_id(0), pl.program_id(1)
    sum_ = None
    for j in range(0, CHUNK, 2):
        at = block * TOPK + part * CHUNK + j
        w = jnp.concatenate([probs_ref[0, j], probs_ref[0, j + 1]], axis=1)
        v = jnp.concatenate([values_ref[owner_ref[at]], values_ref[owner_ref[at + 1]]], axis=0)
        term = jnp.dot(w, v, preferred_element_type=jnp.float32)
        sum_ = term if sum_ is None else sum_ + term

    @pl.when(part == 0)
    def _():
        acc[...] = sum_

    @pl.when(part > 0)
    def _():
        acc[...] += sum_

    @pl.when(part == TOPK // CHUNK - 1)
    def _():
        out = (acc[...] * total_ref[0] + local_ref[0]).astype(jnp.bfloat16)
        for g in range(GROUP):
            out_ref[:, pl.ds(g * HD, HD)] = out[g * QB : (g + 1) * QB]


def mix(owner, probs, values, total, local):
    rows = GROUP * QB
    return pl.pallas_call(
        mix_kernel,
        out_shape=jax.ShapeDtypeStruct((2 * QB, GROUP * HD), jnp.bfloat16),
        grid_spec=pltpu.PrefetchScalarGridSpec(
            num_scalar_prefetch=1,
            grid=(2, TOPK // CHUNK),
            in_specs=[
                pl.BlockSpec((1, CHUNK, rows, BL), lambda b, c, *_: (b, c, 0, 0)),
                pl.BlockSpec(values.shape, lambda b, c, *_: (0, 0, 0)),
                pl.BlockSpec((1, rows, HD), lambda b, c, *_: (b, 0, 0)),
                pl.BlockSpec((1, rows, HD), lambda b, c, *_: (b, 0, 0)),
            ],
            out_specs=pl.BlockSpec((QB, GROUP * HD), lambda b, c, *_: (b, 0)),
            scratch_shapes=[pltpu.VMEM((rows, HD), jnp.float32)],
        ),
        name="mix",
    )(owner, probs, values, total, local)


def per_device(
    queries, local_keys, local_values, memory_keys, memory_values, block_ids, mixing_offset_per_head
):
    owners = lax.axis_size("mem")
    heads = lax.axis_size("head")
    here = memory_keys.shape[0] // BL
    mem_index = lax.axis_index("mem")
    head_index = lax.axis_index("head")

    ids = block_ids.reshape(-1)
    owner = ids // here
    asked = jnp.arange(owners, dtype=jnp.int32)[:, None] == owner[None, :]
    request = jnp.max(jnp.where(asked, (ids % here)[None, :], 0), axis=1)
    wanted = lax.all_to_all(request, "mem", split_axis=0, concat_axis=0, tiled=True)
    key_blocks = gather_blocks(wanted, memory_keys.reshape(here, BL, HD))
    value_blocks = gather_blocks(wanted, memory_values.reshape(here, BL, HD))
    keys = lax.all_to_all(key_blocks, "mem", split_axis=0, concat_axis=0, tiled=True)

    rows = queries.shape[0]
    packed = jnp.concatenate(
        [
            queries.reshape(rows, heads, -1),
            local_keys.reshape(rows, heads, -1),
            local_values.reshape(rows, heads, -1),
        ],
        axis=2,
    ).transpose(1, 0, 2)
    parts = []
    for d in range(heads):
        mine = lax.dynamic_index_in_dim(packed, (head_index + d) % heads, 0, keepdims=False)
        if d:
            mine = lax.ppermute(mine, "head", [(i, (i + d) % heads) for i in range(heads)])
        parts.append(mine)
    qkv = jnp.stack(parts)
    before = lax.ppermute(
        qkv[:, :, GROUP * HD :], "mem", [(i, i + 1) for i in range(owners - 1)]
    )

    values = lax.all_to_all(value_blocks, "mem", split_axis=0, concat_axis=0, tiled=True)

    gate = jax.nn.sigmoid(mixing_offset_per_head)
    place = jnp.stack([mem_index, head_index]).astype(jnp.int32)
    probs, total, local = scores(owner, place, gate, qkv, before, keys)
    out = mix(owner, probs, values, total, local)
    return lax.all_to_all(out, "head", split_axis=0, concat_axis=1, tiled=True)


def solution(mesh):
    return jax.shard_map(
        per_device,
        mesh=mesh,
        in_specs=(
            P(("mem", "head"), None),
            P(("mem", "head"), None),
            P(("mem", "head"), None),
            P("mem", "head"),
            P("mem", "head"),
            P("mem", "head", None),
            P("head"),
        ),
        out_specs=P(("mem", "head"), None),
        check_vma=False,
    )
```

```python
import functools
import math

import jax
import jax.numpy as jnp
from jax import lax
from jax.experimental import pallas as pl
from jax.experimental.pallas import tpu as pltpu
from jax.sharding import PartitionSpec as P

HD = 128
QB = 128
BL = 128
TOPK = 32
WINDOW = 256
GROUP = 4
SCALE = 1.0 / math.sqrt(HD)


def gather_kernel(idx_ref, src_ref, out_ref):
    def move(i, carry):
        out_ref[i] = src_ref[idx_ref[pl.program_id(0) * GATHER + i]]
        return carry

    lax.fori_loop(0, GATHER, move, 0, unroll=4)


GATHER = 16


def gather_blocks(idx, src):
    blocks = idx.shape[0]
    return pl.pallas_call(
        gather_kernel,
        out_shape=jax.ShapeDtypeStruct((blocks,) + src.shape[1:], src.dtype),
        grid_spec=pltpu.PrefetchScalarGridSpec(
            num_scalar_prefetch=1,
            grid=(blocks // GATHER,),
            in_specs=[pl.BlockSpec(src.shape, lambda i, *_: (0, 0, 0))],
            out_specs=pl.BlockSpec((GATHER,) + src.shape[1:], lambda i, *_: (i, 0, 0)),
        ),
        compiler_params=pltpu.CompilerParams(vmem_limit_bytes=8 << 20),
        name="gather_blocks",
    )(idx, src)


def score_kernel(
    owner_ref, place_ref, gate_ref, qkv_ref, before_ref, keys_ref,
    probs_ref, total_ref, local_ref,
    q_scr, k_scr, v_scr, s_scr,
):
    block = pl.program_id(0)
    mem_index, head_index = place_ref[0], place_ref[1]

    @pl.when(block == 0)
    def _():
        for i in range(8):
            at = lax.rem(head_index + 8 - i, 8)
            rows = pl.ds(i * 32, 32)
            for g in range(GROUP):
                q_scr[g, rows, :] = qkv_ref[at, :, pl.ds(g * HD, HD)]
            k_scr[pl.ds(WINDOW + i * 32, 32), :] = qkv_ref[at, :, pl.ds(4 * HD, HD)]
            v_scr[pl.ds(WINDOW + i * 32, 32), :] = qkv_ref[at, :, pl.ds(5 * HD, HD)]
            k_scr[pl.ds(i * 32, 32), :] = before_ref[at, :, pl.ds(0, HD)]
            v_scr[pl.ds(i * 32, 32), :] = before_ref[at, :, pl.ds(HD, HD)]

    start = pl.multiple_of(block * QB, QB)
    q = q_scr[:, pl.ds(start, QB), :].reshape(GROUP * QB, HD)

    span = WINDOW + QB
    lk = k_scr[pl.ds(start, span), :]
    lv = v_scr[pl.ds(start, span), :]
    ls = lax.dot_general(q, lk, (((1,), (1,)), ((), ())), preferred_element_type=jnp.float32) * SCALE
    t = lax.broadcasted_iota(jnp.int32, (QB, span), 0)
    s = lax.broadcasted_iota(jnp.int32, (QB, span), 1)
    apart = t + WINDOW - s
    known = mem_index * (2 * QB) + block * QB - WINDOW + s >= 0
    allowed = known & (apart >= 0) & (apart < WINDOW)
    ls = jnp.where(allowed[None], ls.reshape(GROUP, QB, span), -1e30).reshape(GROUP * QB, span)
    lm = jnp.max(ls, axis=1, keepdims=True)
    lw = jnp.exp(ls - lm)
    lt = jnp.sum(lw, axis=1, keepdims=True)
    lo = jnp.dot(lw.astype(jnp.bfloat16), lv, preferred_element_type=jnp.float32) / lt
    for g in range(GROUP):
        rows = pl.ds(g * QB, QB)
        local_ref[0, rows, :] = lo[g * QB : (g + 1) * QB] * (1.0 - gate_ref[g])

    def score(j, high):
        sc = lax.dot_general(
            q, keys_ref[owner_ref[block * TOPK + j]], (((1,), (1,)), ((), ())),
            preferred_element_type=jnp.float32,
        ) * SCALE
        s_scr[j] = sc
        return jnp.maximum(high, sc)

    high = lax.fori_loop(0, TOPK, score, jnp.full((GROUP * QB, BL), -jnp.inf, jnp.float32))
    high = jnp.broadcast_to(jnp.max(high, axis=1, keepdims=True), (GROUP * QB, BL))

    def weigh(j, total):
        w = jnp.exp(s_scr[j] - high)
        probs_ref[0, j] = w.astype(jnp.bfloat16)
        return total + w

    total = lax.fori_loop(0, TOPK, weigh, jnp.zeros((GROUP * QB, BL), jnp.float32))
    total = jnp.broadcast_to(jnp.sum(total, axis=1, keepdims=True), (GROUP * QB, BL))
    for g in range(GROUP):
        rows = pl.ds(g * QB, QB)
        total_ref[0, rows, :] = gate_ref[g] / total[g * QB : (g + 1) * QB]


def scores(owner, place, gate, qkv, before, keys):
    whole = lambda shape: pl.BlockSpec(shape, lambda b, *_: (0,) * len(shape))
    rows = GROUP * QB
    return pl.pallas_call(
        score_kernel,
        out_shape=(
            jax.ShapeDtypeStruct((2, TOPK, rows, BL), jnp.bfloat16),
            jax.ShapeDtypeStruct((2, rows, HD), jnp.float32),
            jax.ShapeDtypeStruct((2, rows, HD), jnp.float32),
        ),
        grid_spec=pltpu.PrefetchScalarGridSpec(
            num_scalar_prefetch=3,
            grid=(2,),
            in_specs=[whole(qkv.shape), whole(before.shape), whole(keys.shape)],
            out_specs=(
                pl.BlockSpec((1, TOPK, rows, BL), lambda b, *_: (b, 0, 0, 0)),
                pl.BlockSpec((1, rows, HD), lambda b, *_: (b, 0, 0)),
                pl.BlockSpec((1, rows, HD), lambda b, *_: (b, 0, 0)),
            ),
            scratch_shapes=[
                pltpu.VMEM((GROUP, 2 * QB, HD), jnp.bfloat16),
                pltpu.VMEM((WINDOW + 2 * QB, HD), jnp.bfloat16),
                pltpu.VMEM((WINDOW + 2 * QB, HD), jnp.bfloat16),
                pltpu.VMEM((TOPK, rows, BL), jnp.float32),
            ],
        ),
        compiler_params=pltpu.CompilerParams(vmem_limit_bytes=30 << 20),
        name="scores",
    )(owner, place, gate, qkv, before, keys)


CHUNK = 8


def mix_kernel(owner_ref, probs_ref, values_ref, total_ref, local_ref, out_ref, acc):
    block, part = pl.program_id(0), pl.program_id(1)
    sum_ = None
    for j in range(0, CHUNK, 2):
        at = block * TOPK + part * CHUNK + j
        w = jnp.concatenate([probs_ref[0, j], probs_ref[0, j + 1]], axis=1)
        v = jnp.concatenate([values_ref[owner_ref[at]], values_ref[owner_ref[at + 1]]], axis=0)
        term = jnp.dot(w, v, preferred_element_type=jnp.float32)
        sum_ = term if sum_ is None else sum_ + term

    @pl.when(part == 0)
    def _():
        acc[...] = sum_

    @pl.when(part > 0)
    def _():
        acc[...] += sum_

    @pl.when(part == TOPK // CHUNK - 1)
    def _():
        out = (acc[...] * total_ref[0] + local_ref[0]).astype(jnp.bfloat16)
        for g in range(GROUP):
            out_ref[:, pl.ds(g * HD, HD)] = out[g * QB : (g + 1) * QB]


def mix(owner, probs, values, total, local):
    rows = GROUP * QB
    return pl.pallas_call(
        mix_kernel,
        out_shape=jax.ShapeDtypeStruct((2 * QB, GROUP * HD), jnp.bfloat16),
        grid_spec=pltpu.PrefetchScalarGridSpec(
            num_scalar_prefetch=1,
            grid=(2, TOPK // CHUNK),
            in_specs=[
                pl.BlockSpec((1, CHUNK, rows, BL), lambda b, c, *_: (b, c, 0, 0)),
                pl.BlockSpec(values.shape, lambda b, c, *_: (0, 0, 0)),
                pl.BlockSpec((1, rows, HD), lambda b, c, *_: (b, 0, 0)),
                pl.BlockSpec((1, rows, HD), lambda b, c, *_: (b, 0, 0)),
            ],
            out_specs=pl.BlockSpec((QB, GROUP * HD), lambda b, c, *_: (b, 0)),
            scratch_shapes=[pltpu.VMEM((rows, HD), jnp.float32)],
        ),
        compiler_params=pltpu.CompilerParams(vmem_limit_bytes=16 << 20),
        name="mix",
    )(owner, probs, values, total, local)


def per_device(
    queries, local_keys, local_values, memory_keys, memory_values, block_ids, mixing_offset_per_head
):
    owners = lax.axis_size("mem")
    heads = lax.axis_size("head")
    here = memory_keys.shape[0] // BL
    mem_index = lax.axis_index("mem")
    head_index = lax.axis_index("head")

    ids = block_ids.reshape(-1)
    owner = ids // here
    asked = jnp.arange(owners, dtype=jnp.int32)[:, None] == owner[None, :]
    request = jnp.max(jnp.where(asked, (ids % here)[None, :], 0), axis=1)
    wanted = lax.all_to_all(request, "mem", split_axis=0, concat_axis=0, tiled=True)
    key_blocks = gather_blocks(wanted, memory_keys.reshape(here, BL, HD))
    value_blocks = gather_blocks(wanted, memory_values.reshape(here, BL, HD))
    keys = lax.all_to_all(key_blocks, "mem", split_axis=0, concat_axis=0, tiled=True)

    rows = queries.shape[0]
    packed = jnp.concatenate(
        [
            queries.reshape(rows, heads, -1),
            local_keys.reshape(rows, heads, -1),
            local_values.reshape(rows, heads, -1),
        ],
        axis=2,
    ).transpose(1, 0, 2)
    parts = []
    for d in range(heads):
        mine = lax.dynamic_index_in_dim(packed, (head_index + d) % heads, 0, keepdims=False)
        if d:
            mine = lax.ppermute(mine, "head", [(i, (i + d) % heads) for i in range(heads)])
        parts.append(mine)
    qkv = jnp.stack(parts)
    before = lax.ppermute(
        qkv[:, :, GROUP * HD :], "mem", [(i, i + 1) for i in range(owners - 1)]
    )

    value_blocks, qkv = lax.optimization_barrier((value_blocks, qkv))
    values = lax.all_to_all(value_blocks, "mem", split_axis=0, concat_axis=0, tiled=True)

    gate = jax.nn.sigmoid(mixing_offset_per_head)
    place = jnp.stack([mem_index, head_index]).astype(jnp.int32)
    probs, total, local = scores(owner, place, gate, qkv, before, keys)
    out = mix(owner, probs, values, total, local)
    return lax.all_to_all(out, "head", split_axis=0, concat_axis=1, tiled=True)


def solution(mesh):
    return jax.shard_map(
        per_device,
        mesh=mesh,
        in_specs=(
            P(("mem", "head"), None),
            P(("mem", "head"), None),
            P(("mem", "head"), None),
            P("mem", "head"),
            P("mem", "head"),
            P("mem", "head", None),
            P("head"),
        ),
        out_specs=P(("mem", "head"), None),
        check_vma=False,
    )
```

```python
import functools
import math

import jax
import jax.numpy as jnp
from jax import lax
from jax.experimental import pallas as pl
from jax.experimental.pallas import tpu as pltpu
from jax.sharding import PartitionSpec as P

HD = 128
QB = 128
BL = 128
TOPK = 32
WINDOW = 256
GROUP = 4
SCALE = 1.0 / math.sqrt(HD)


GATHER = 16


def gather_kernel(idx_ref, keys_ref, values_ref, out_ref):
    def move(i, carry):
        at = idx_ref[pl.program_id(0) * GATHER + i]
        out_ref[i, 0] = keys_ref[at]
        out_ref[i, 1] = values_ref[at]
        return carry

    lax.fori_loop(0, GATHER, move, 0, unroll=4)


def gather_blocks(idx, keys, values):
    blocks = idx.shape[0]
    whole = pl.BlockSpec(keys.shape, lambda i, *_: (0, 0, 0))
    return pl.pallas_call(
        gather_kernel,
        out_shape=jax.ShapeDtypeStruct((blocks, 2) + keys.shape[1:], keys.dtype),
        grid_spec=pltpu.PrefetchScalarGridSpec(
            num_scalar_prefetch=1,
            grid=(blocks // GATHER,),
            in_specs=[whole, whole],
            out_specs=pl.BlockSpec((GATHER, 2) + keys.shape[1:], lambda i, *_: (i, 0, 0, 0)),
        ),
        compiler_params=pltpu.CompilerParams(vmem_limit_bytes=12 << 20),
        name="gather_blocks",
    )(idx, keys, values)


def assemble_kernel(place_ref, *refs):
    parts, (q_ref, kv_ref) = refs[:8], refs[8:]
    for d in range(8):
        rows = pl.ds(pl.multiple_of(lax.rem(place_ref[1] + 8 - d, 8) * 32, 32), 32)
        for g in range(GROUP):
            q_ref[g, rows, :] = parts[d][:, pl.ds(g * HD, HD)]
        kv_ref[0, rows, :] = parts[d][:, pl.ds(4 * HD, HD)]
        kv_ref[1, rows, :] = parts[d][:, pl.ds(5 * HD, HD)]


def whole_spec(shape):
    return pl.BlockSpec(shape, lambda b, *_: (0,) * len(shape))


def assemble(place, parts):
    shapes = ((GROUP, 2 * QB, HD), (2, 2 * QB, HD))
    return pl.pallas_call(
        assemble_kernel,
        out_shape=tuple(jax.ShapeDtypeStruct(shape, jnp.bfloat16) for shape in shapes),
        grid_spec=pltpu.PrefetchScalarGridSpec(
            num_scalar_prefetch=1,
            grid=(1,),
            in_specs=[whole_spec(part.shape) for part in parts],
            out_specs=tuple(whole_spec(shape) for shape in shapes),
        ),
        compiler_params=pltpu.CompilerParams(vmem_limit_bytes=8 << 20),
        name="assemble",
    )(place, *parts)


def local_kernel(place_ref, gate_ref, q_ref, own_ref, before_ref, out_ref):
    block = pl.program_id(0)
    rows_here = GROUP * QB
    span = WINDOW + QB
    start = pl.multiple_of(block * QB, QB)
    q = q_ref[...].reshape(rows_here, HD)
    k = jnp.concatenate([before_ref[0], own_ref[0]], axis=0)
    v = jnp.concatenate([before_ref[1], own_ref[1]], axis=0)
    k = jnp.where(block == 0, k[:span], k[QB:])
    v = jnp.where(block == 0, v[:span], v[QB:])
    sc = lax.dot_general(q, k, (((1,), (1,)), ((), ())), preferred_element_type=jnp.float32) * SCALE
    t = lax.broadcasted_iota(jnp.int32, (QB, span), 0)
    s = lax.broadcasted_iota(jnp.int32, (QB, span), 1)
    apart = t + WINDOW - s
    known = place_ref[0] * (2 * QB) + start - WINDOW + s >= 0
    allowed = known & (apart >= 0) & (apart < WINDOW)
    sc = jnp.where(allowed[None], sc.reshape(GROUP, QB, span), -1e30).reshape(rows_here, span)
    w = jnp.exp(sc - jnp.max(sc, axis=1, keepdims=True))
    total = jnp.sum(w, axis=1, keepdims=True)
    out = jnp.dot(w.astype(jnp.bfloat16), v, preferred_element_type=jnp.float32) / total
    for g in range(GROUP):
        out_ref[0, pl.ds(g * QB, QB), :] = out[g * QB : (g + 1) * QB] * (1.0 - gate_ref[g])


def local_attention(place, gate, q, own, before):
    return pl.pallas_call(
        local_kernel,
        out_shape=jax.ShapeDtypeStruct((2, GROUP * QB, HD), jnp.float32),
        grid_spec=pltpu.PrefetchScalarGridSpec(
            num_scalar_prefetch=2,
            grid=(2,),
            in_specs=[
                pl.BlockSpec((GROUP, QB, HD), lambda b, *_: (0, b, 0)),
                whole_spec(own.shape),
                whole_spec(before.shape),
            ],
            out_specs=pl.BlockSpec((1, GROUP * QB, HD), lambda b, *_: (b, 0, 0)),
        ),
        compiler_params=pltpu.CompilerParams(vmem_limit_bytes=12 << 20),
        name="local",
    )(place, gate, q, own, before)


PAIRS = TOPK // 2


def attend_kernel(owner_ref, gate_ref, q_ref, mem_ref, local_ref, out_ref, s_scr, high, total, acc):
    block = pl.program_id(0)
    rows_here = GROUP * QB
    q = q_ref[...].reshape(rows_here, HD)
    high[...] = jnp.full((rows_here, HD), -jnp.inf, jnp.float32)
    total[...] = jnp.zeros((rows_here, HD), jnp.float32)
    acc[...] = jnp.zeros((rows_here, HD), jnp.float32)

    def pair(i, which):
        at = block * TOPK + 2 * i
        return jnp.concatenate(
            [mem_ref[owner_ref[at], which], mem_ref[owner_ref[at + 1], which]], axis=0
        )

    def score(i, carry):
        sc = lax.dot_general(
            q, pair(i, 0), (((1,), (1,)), ((), ())), preferred_element_type=jnp.float32
        )
        s_scr[i] = sc
        high[...] = jnp.maximum(high[...], jnp.maximum(sc[:, :HD], sc[:, HD:]))
        return carry

    lax.fori_loop(0, PAIRS, score, 0, unroll=4)
    high[...] = jnp.broadcast_to(jnp.max(high[...], axis=1, keepdims=True) * SCALE, (rows_here, HD))

    def weigh(i, carry):
        top = high[...]
        left = jnp.exp(s_scr[i, :, :HD] * SCALE - top)
        right = jnp.exp(s_scr[i, :, HD:] * SCALE - top)
        total[...] += left + right
        w = jnp.concatenate([left.astype(jnp.bfloat16), right.astype(jnp.bfloat16)], axis=1)
        acc[...] += jnp.dot(w, pair(i, 1), preferred_element_type=jnp.float32)
        return carry

    lax.fori_loop(0, PAIRS, weigh, 0, unroll=4)
    out = acc[...] / jnp.sum(total[...], axis=1, keepdims=True)
    for g in range(GROUP):
        rows = slice(g * QB, (g + 1) * QB)
        out_ref[:, pl.ds(g * HD, HD)] = (out[rows] * gate_ref[g] + local_ref[0, rows]).astype(jnp.bfloat16)


def attend(owner, gate, q, mem, local):
    rows = GROUP * QB
    return pl.pallas_call(
        attend_kernel,
        out_shape=jax.ShapeDtypeStruct((2 * QB, GROUP * HD), jnp.bfloat16),
        grid_spec=pltpu.PrefetchScalarGridSpec(
            num_scalar_prefetch=2,
            grid=(2,),
            in_specs=[
                pl.BlockSpec((GROUP, QB, HD), lambda b, *_: (0, b, 0)),
                whole_spec(mem.shape),
                pl.BlockSpec((1, rows, HD), lambda b, *_: (b, 0, 0)),
            ],
            out_specs=pl.BlockSpec((QB, GROUP * HD), lambda b, *_: (b, 0)),
            scratch_shapes=[pltpu.VMEM((PAIRS, rows, 2 * BL), jnp.float32)]
            + [pltpu.VMEM((rows, HD), jnp.float32)] * 3,
        ),
        compiler_params=pltpu.CompilerParams(vmem_limit_bytes=36 << 20),
        name="attend",
    )(owner, gate, q, mem, local)


def per_device(
    queries, local_keys, local_values, memory_keys, memory_values, block_ids, mixing_offset_per_head
):
    owners = lax.axis_size("mem")
    heads = lax.axis_size("head")
    here = memory_keys.shape[0] // BL
    mem_index = lax.axis_index("mem")
    head_index = lax.axis_index("head")

    ids = block_ids.reshape(-1)
    owner = ids // here
    asked = jnp.arange(owners, dtype=jnp.int32)[:, None] == owner[None, :]
    request = jnp.max(jnp.where(asked, (ids % here)[None, :], 0), axis=1)
    wanted = lax.all_to_all(request, "mem", split_axis=0, concat_axis=0, tiled=True)
    blocks = gather_blocks(
        wanted, memory_keys.reshape(here, BL, HD), memory_values.reshape(here, BL, HD)
    )
    mem = lax.all_to_all(blocks, "mem", split_axis=0, concat_axis=0, tiled=True)

    rows = queries.shape[0]
    packed = jnp.concatenate(
        [
            queries.reshape(rows, heads, -1),
            local_keys.reshape(rows, heads, -1),
            local_values.reshape(rows, heads, -1),
        ],
        axis=2,
    ).transpose(1, 0, 2)
    parts = []
    for d in range(heads):
        mine = lax.dynamic_index_in_dim(packed, (head_index + d) % heads, 0, keepdims=False)
        if d:
            mine = lax.ppermute(mine, "head", [(i, (i + d) % heads) for i in range(heads)])
        parts.append(mine)
    place = jnp.stack([mem_index, head_index]).astype(jnp.int32)
    q, own = assemble(place, parts)
    before = lax.ppermute(own, "mem", [(i, i + 1) for i in range(owners - 1)])
    gate = jax.nn.sigmoid(mixing_offset_per_head)
    local = local_attention(place, gate, q, own, before)
    out = attend(owner, gate, q, mem, local)
    return lax.all_to_all(out, "head", split_axis=0, concat_axis=1, tiled=True)


def solution(mesh):
    return jax.shard_map(
        per_device,
        mesh=mesh,
        in_specs=(
            P(("mem", "head"), None),
            P(("mem", "head"), None),
            P(("mem", "head"), None),
            P("mem", "head"),
            P("mem", "head"),
            P("mem", "head", None),
            P("head"),
        ),
        out_specs=P(("mem", "head"), None),
        check_vma=False,
    )
```

```python
import functools
import math

import jax
import jax.numpy as jnp
from jax import lax
from jax.experimental import pallas as pl
from jax.experimental.pallas import tpu as pltpu
from jax.sharding import PartitionSpec as P

HD = 128
QB = 128
BL = 128
TOPK = 32
WINDOW = 256
GROUP = 4
OWNERS = 64
HERE = 32
SCALE = 1.0 / math.sqrt(HD)


def request_kernel(ids_ref, out_ref):
    out_ref[...] = jnp.zeros_like(out_ref)

    def ask(i, carry):
        at = ids_ref[i // TOPK, 0, lax.rem(i, TOPK)]
        out_ref[pl.ds(at // HERE, 1), :] = jnp.full((1, 128), lax.rem(at, HERE), jnp.int32)
        return carry

    lax.fori_loop(0, 2 * TOPK, ask, 0, unroll=8)


def requests(ids):
    return pl.pallas_call(
        request_kernel,
        out_shape=jax.ShapeDtypeStruct((OWNERS, 128), jnp.int32),
        grid_spec=pltpu.PrefetchScalarGridSpec(
            num_scalar_prefetch=1,
            grid=(1,),
            in_specs=[],
            out_specs=pl.BlockSpec((OWNERS, 128), lambda i, *_: (0, 0)),
        ),
        compiler_params=pltpu.CompilerParams(vmem_limit_bytes=4 << 20),
        name="requests",
    )(ids)


PARTS = 4


def gather_kernel(idx_ref, keys_ref, values_ref, out_ref, buf, load_sem, store_sem):
    count = OWNERS // PARTS

    def load(part):
        def move(i, carry):
            at = idx_ref[part * count + i, 0]
            to = part * count + i
            pltpu.make_async_copy(keys_ref.at[at], buf.at[to, 0], load_sem.at[part]).start()
            pltpu.make_async_copy(values_ref.at[at], buf.at[to, 1], load_sem.at[part]).start()
            return carry

        lax.fori_loop(0, count, move, 0, unroll=4)

    def store(part):
        rows = pl.ds(part * count, count)
        return pltpu.make_async_copy(buf.at[rows], out_ref.at[rows], store_sem.at[part])

    for part in range(PARTS):
        load(part)
    for part in range(PARTS):
        rows = pl.ds(part * count, count)
        pltpu.make_async_copy(buf.at[rows], buf.at[rows], load_sem.at[part]).wait()
        store(part).start()
    for part in range(PARTS):
        store(part).wait()


def gather_blocks(idx, keys, values):
    shape = (OWNERS, 2) + keys.shape[1:]
    return pl.pallas_call(
        gather_kernel,
        out_shape=jax.ShapeDtypeStruct(shape, keys.dtype),
        grid_spec=pltpu.PrefetchScalarGridSpec(
            num_scalar_prefetch=1,
            grid=(1,),
            in_specs=[pl.BlockSpec(memory_space=pltpu.HBM)] * 2,
            out_specs=pl.BlockSpec(memory_space=pltpu.HBM),
            scratch_shapes=[
                pltpu.VMEM(shape, keys.dtype),
                pltpu.SemaphoreType.DMA((PARTS,)),
                pltpu.SemaphoreType.DMA((PARTS,)),
            ],
        ),
        compiler_params=pltpu.CompilerParams(vmem_limit_bytes=62 << 20),
        name="gather_blocks",
    )(idx, keys, values)


def assemble_kernel(place_ref, *refs):
    parts, (q_ref, kv_ref) = refs[:8], refs[8:]
    for d in range(8):
        rows = pl.ds(pl.multiple_of(lax.rem(place_ref[1] + 8 - d, 8) * 32, 32), 32)
        for g in range(GROUP):
            q_ref[g, rows, :] = parts[d][:, pl.ds(g * HD, HD)]
        kv_ref[0, rows, :] = parts[d][:, pl.ds(4 * HD, HD)]
        kv_ref[1, rows, :] = parts[d][:, pl.ds(5 * HD, HD)]


def whole_spec(shape):
    return pl.BlockSpec(shape, lambda b, *_: (0,) * len(shape))


def assemble(place, parts):
    shapes = ((GROUP, 2 * QB, HD), (2, 2 * QB, HD))
    return pl.pallas_call(
        assemble_kernel,
        out_shape=tuple(jax.ShapeDtypeStruct(shape, jnp.bfloat16) for shape in shapes),
        grid_spec=pltpu.PrefetchScalarGridSpec(
            num_scalar_prefetch=1,
            grid=(1,),
            in_specs=[whole_spec(part.shape) for part in parts],
            out_specs=tuple(whole_spec(shape) for shape in shapes),
        ),
        compiler_params=pltpu.CompilerParams(vmem_limit_bytes=8 << 20),
        name="assemble",
    )(place, *parts)


def local_kernel(place_ref, gate_ref, q_ref, own_ref, before_ref, out_ref):
    block = pl.program_id(0)
    rows_here = GROUP * QB
    span = WINDOW + QB
    start = pl.multiple_of(block * QB, QB)
    q = q_ref[...].reshape(rows_here, HD)
    k = jnp.concatenate([before_ref[0], own_ref[0]], axis=0)
    v = jnp.concatenate([before_ref[1], own_ref[1]], axis=0)
    k = jnp.where(block == 0, k[:span], k[QB:])
    v = jnp.where(block == 0, v[:span], v[QB:])
    sc = lax.dot_general(q, k, (((1,), (1,)), ((), ())), preferred_element_type=jnp.float32) * SCALE
    t = lax.broadcasted_iota(jnp.int32, (QB, span), 0)
    s = lax.broadcasted_iota(jnp.int32, (QB, span), 1)
    apart = t + WINDOW - s
    known = place_ref[0] * (2 * QB) + start - WINDOW + s >= 0
    allowed = known & (apart >= 0) & (apart < WINDOW)
    sc = jnp.where(allowed[None], sc.reshape(GROUP, QB, span), -1e30).reshape(rows_here, span)
    w = jnp.exp(sc - jnp.max(sc, axis=1, keepdims=True))
    total = jnp.sum(w, axis=1, keepdims=True)
    out = jnp.dot(w.astype(jnp.bfloat16), v, preferred_element_type=jnp.float32) / total
    for g in range(GROUP):
        out_ref[0, pl.ds(g * QB, QB), :] = out[g * QB : (g + 1) * QB] * (1.0 - gate_ref[g])


def local_attention(place, gate, q, own, before):
    return pl.pallas_call(
        local_kernel,
        out_shape=jax.ShapeDtypeStruct((2, GROUP * QB, HD), jnp.float32),
        grid_spec=pltpu.PrefetchScalarGridSpec(
            num_scalar_prefetch=2,
            grid=(2,),
            in_specs=[
                pl.BlockSpec((GROUP, QB, HD), lambda b, *_: (0, b, 0)),
                whole_spec(own.shape),
                whole_spec(before.shape),
            ],
            out_specs=pl.BlockSpec((1, GROUP * QB, HD), lambda b, *_: (b, 0, 0)),
        ),
        compiler_params=pltpu.CompilerParams(vmem_limit_bytes=12 << 20),
        name="local",
    )(place, gate, q, own, before)


STEP = 4
STEPS = TOPK // STEP
WIDE = STEP * BL
LOG2E = math.log2(math.e)


def attend_kernel(ids_ref, gate_ref, q_ref, mem_ref, local_ref, out_ref, s_scr, high, total, acc):
    block = pl.program_id(0)
    rows_here = GROUP * QB
    q = q_ref[...].reshape(rows_here, HD)
    high[...] = jnp.full((rows_here, HD), -jnp.inf, jnp.float32)
    total[...] = jnp.zeros((rows_here, HD), jnp.float32)
    acc[...] = jnp.zeros((rows_here, HD), jnp.float32)

    def some(i, which):
        return jnp.concatenate(
            [mem_ref[ids_ref[block, 0, STEP * i + j] // HERE, which] for j in range(STEP)], axis=0
        )

    def fold(op, x):
        out = x[:, :HD]
        for j in range(1, STEP):
            out = op(out, x[:, j * HD : (j + 1) * HD])
        return out

    def score(i, carry):
        sc = lax.dot_general(
            q, some(i, 0), (((1,), (1,)), ((), ())), preferred_element_type=jnp.float32
        )
        s_scr[i] = sc
        high[...] = jnp.maximum(high[...], fold(jnp.maximum, sc))
        return carry

    lax.fori_loop(0, STEPS, score, 0, unroll=2)
    factor = SCALE * LOG2E
    high[...] = jnp.broadcast_to(jnp.max(high[...], axis=1, keepdims=True) * factor, (rows_here, HD))

    def weigh(i, carry):
        top = high[...]
        w = [jnp.exp2(s_scr[i, :, j * HD : (j + 1) * HD] * factor - top) for j in range(STEP)]
        total[...] += (w[0] + w[1]) + (w[2] + w[3])
        w = jnp.concatenate([one.astype(jnp.bfloat16) for one in w], axis=1)
        acc[...] += jnp.dot(w, some(i, 1), preferred_element_type=jnp.float32)
        return carry

    lax.fori_loop(0, STEPS, weigh, 0, unroll=2)
    out = acc[...] / jnp.sum(total[...], axis=1, keepdims=True)
    for g in range(GROUP):
        rows = slice(g * QB, (g + 1) * QB)
        out_ref[:, pl.ds(g * HD, HD)] = (out[rows] * gate_ref[g] + local_ref[0, rows]).astype(jnp.bfloat16)


def attend(ids, gate, q, mem, local):
    rows = GROUP * QB
    return pl.pallas_call(
        attend_kernel,
        out_shape=jax.ShapeDtypeStruct((2 * QB, GROUP * HD), jnp.bfloat16),
        grid_spec=pltpu.PrefetchScalarGridSpec(
            num_scalar_prefetch=2,
            grid=(2,),
            in_specs=[
                pl.BlockSpec((GROUP, QB, HD), lambda b, *_: (0, b, 0)),
                whole_spec(mem.shape),
                pl.BlockSpec((1, rows, HD), lambda b, *_: (b, 0, 0)),
            ],
            out_specs=pl.BlockSpec((QB, GROUP * HD), lambda b, *_: (b, 0)),
            scratch_shapes=[pltpu.VMEM((STEPS, rows, WIDE), jnp.float32)]
            + [pltpu.VMEM((rows, HD), jnp.float32)] * 3,
        ),
        compiler_params=pltpu.CompilerParams(vmem_limit_bytes=36 << 20),
        name="attend",
    )(ids, gate, q, mem, local)


def per_device(
    queries, local_keys, local_values, memory_keys, memory_values, block_ids, mixing_offset_per_head
):
    owners = lax.axis_size("mem")
    heads = lax.axis_size("head")
    here = memory_keys.shape[0] // BL
    mem_index = lax.axis_index("mem")
    head_index = lax.axis_index("head")

    wanted = lax.all_to_all(requests(block_ids), "mem", split_axis=0, concat_axis=0, tiled=True)
    blocks = gather_blocks(
        wanted, memory_keys.reshape(here, BL, HD), memory_values.reshape(here, BL, HD)
    )
    mem = lax.all_to_all(blocks, "mem", split_axis=0, concat_axis=0, tiled=True)

    rows = queries.shape[0]
    packed = jnp.concatenate(
        [
            queries.reshape(rows, heads, -1),
            local_keys.reshape(rows, heads, -1),
            local_values.reshape(rows, heads, -1),
        ],
        axis=2,
    ).transpose(1, 0, 2)
    parts = []
    for d in range(heads):
        mine = lax.dynamic_index_in_dim(packed, (head_index + d) % heads, 0, keepdims=False)
        if d:
            mine = lax.ppermute(mine, "head", [(i, (i + d) % heads) for i in range(heads)])
        parts.append(mine)
    place = jnp.stack([mem_index, head_index]).astype(jnp.int32)
    q, own = assemble(place, parts)
    before = lax.ppermute(own, "mem", [(i, i + 1) for i in range(owners - 1)])
    gate = jax.nn.sigmoid(mixing_offset_per_head)
    local = local_attention(place, gate, q, own, before)
    out = attend(block_ids, gate, q, mem, local)
    return lax.all_to_all(out, "head", split_axis=0, concat_axis=1, tiled=True)


def solution(mesh):
    return jax.shard_map(
        per_device,
        mesh=mesh,
        in_specs=(
            P(("mem", "head"), None),
            P(("mem", "head"), None),
            P(("mem", "head"), None),
            P("mem", "head"),
            P("mem", "head"),
            P("mem", "head", None),
            P("head"),
        ),
        out_specs=P(("mem", "head"), None),
        check_vma=False,
    )
```

```python
import functools
import math

import jax
import jax.numpy as jnp
from jax import lax
from jax.experimental import pallas as pl
from jax.experimental.pallas import tpu as pltpu
from jax.sharding import PartitionSpec as P

HD = 128
QB = 128
BL = 128
TOPK = 32
WINDOW = 256
GROUP = 4
OWNERS = 64
HERE = 32
SCALE = 1.0 / math.sqrt(HD)


def owner_of(block):
    return lax.shift_right_logical(block, 5)


def request_kernel(ids_ref, out_ref):
    out_ref[...] = jnp.zeros_like(out_ref)

    def ask(i, carry):
        for block in range(2):
            at = ids_ref[block, 0, i]
            out_ref[pl.ds(owner_of(at), 1), :] = jnp.full((1, 128), at & (HERE - 1), jnp.int32)
        return carry

    lax.fori_loop(0, TOPK, ask, 0, unroll=8)


def requests(ids):
    return pl.pallas_call(
        request_kernel,
        out_shape=jax.ShapeDtypeStruct((OWNERS, 128), jnp.int32),
        grid_spec=pltpu.PrefetchScalarGridSpec(
            num_scalar_prefetch=1,
            grid=(1,),
            in_specs=[],
            out_specs=pl.BlockSpec((OWNERS, 128), lambda i, *_: (0, 0)),
        ),
        compiler_params=pltpu.CompilerParams(vmem_limit_bytes=4 << 20),
        name="requests",
    )(ids)


GATHER = 8


def gather_kernel(idx_ref, keys_ref, values_ref, out_ref):
    for i in range(GATHER):
        at = idx_ref[pl.program_id(0) * GATHER + i, 0]
        out_ref[i, 0] = keys_ref[at]
        out_ref[i, 1] = values_ref[at]


def gather_blocks(idx, keys, values):
    whole = pl.BlockSpec(keys.shape, lambda i, *_: (0, 0, 0))
    return pl.pallas_call(
        gather_kernel,
        out_shape=jax.ShapeDtypeStruct((OWNERS, 2) + keys.shape[1:], keys.dtype),
        grid_spec=pltpu.PrefetchScalarGridSpec(
            num_scalar_prefetch=1,
            grid=(OWNERS // GATHER,),
            in_specs=[whole, whole],
            out_specs=pl.BlockSpec((GATHER, 2) + keys.shape[1:], lambda i, *_: (i, 0, 0, 0)),
        ),
        compiler_params=pltpu.CompilerParams(vmem_limit_bytes=62 << 20),
        name="gather_blocks",
    )(idx, keys, values)


def assemble_kernel(place_ref, *refs):
    parts, (q_ref, kv_ref) = refs[:8], refs[8:]
    for d in range(8):
        rows = pl.ds(pl.multiple_of(lax.rem(place_ref[1] + 8 - d, 8) * 32, 32), 32)
        for g in range(GROUP):
            q_ref[g, rows, :] = parts[d][:, pl.ds(g * HD, HD)]
        kv_ref[0, rows, :] = parts[d][:, pl.ds(4 * HD, HD)]
        kv_ref[1, rows, :] = parts[d][:, pl.ds(5 * HD, HD)]


def whole_spec(shape):
    return pl.BlockSpec(shape, lambda b, *_: (0,) * len(shape))


def assemble(place, parts):
    shapes = ((GROUP, 2 * QB, HD), (2, 2 * QB, HD))
    return pl.pallas_call(
        assemble_kernel,
        out_shape=tuple(jax.ShapeDtypeStruct(shape, jnp.bfloat16) for shape in shapes),
        grid_spec=pltpu.PrefetchScalarGridSpec(
            num_scalar_prefetch=1,
            grid=(1,),
            in_specs=[whole_spec(part.shape) for part in parts],
            out_specs=tuple(whole_spec(shape) for shape in shapes),
        ),
        compiler_params=pltpu.CompilerParams(vmem_limit_bytes=8 << 20),
        name="assemble",
    )(place, *parts)


def local_kernel(place_ref, gate_ref, q_ref, own_ref, before_ref, out_ref):
    block = pl.program_id(0)
    rows_here = GROUP * QB
    span = WINDOW + QB
    start = pl.multiple_of(block * QB, QB)
    q = q_ref[...].reshape(rows_here, HD)
    k = jnp.concatenate([before_ref[0], own_ref[0]], axis=0)
    v = jnp.concatenate([before_ref[1], own_ref[1]], axis=0)
    k = jnp.where(block == 0, k[:span], k[QB:])
    v = jnp.where(block == 0, v[:span], v[QB:])
    sc = lax.dot_general(q, k, (((1,), (1,)), ((), ())), preferred_element_type=jnp.float32) * SCALE
    t = lax.broadcasted_iota(jnp.int32, (QB, span), 0)
    s = lax.broadcasted_iota(jnp.int32, (QB, span), 1)
    apart = t + WINDOW - s
    known = place_ref[0] * (2 * QB) + start - WINDOW + s >= 0
    allowed = known & (apart >= 0) & (apart < WINDOW)
    sc = jnp.where(allowed[None], sc.reshape(GROUP, QB, span), -1e30).reshape(rows_here, span)
    w = jnp.exp(sc - jnp.max(sc, axis=1, keepdims=True))
    total = jnp.sum(w, axis=1, keepdims=True)
    out = jnp.dot(w.astype(jnp.bfloat16), v, preferred_element_type=jnp.float32) / total
    for g in range(GROUP):
        out_ref[0, pl.ds(g * QB, QB), :] = out[g * QB : (g + 1) * QB] * (1.0 - gate_ref[g])


def local_attention(place, gate, q, own, before):
    return pl.pallas_call(
        local_kernel,
        out_shape=jax.ShapeDtypeStruct((2, GROUP * QB, HD), jnp.float32),
        grid_spec=pltpu.PrefetchScalarGridSpec(
            num_scalar_prefetch=2,
            grid=(2,),
            in_specs=[
                pl.BlockSpec((GROUP, QB, HD), lambda b, *_: (0, b, 0)),
                whole_spec(own.shape),
                whole_spec(before.shape),
            ],
            out_specs=pl.BlockSpec((1, GROUP * QB, HD), lambda b, *_: (b, 0, 0)),
        ),
        compiler_params=pltpu.CompilerParams(vmem_limit_bytes=12 << 20),
        name="local",
    )(place, gate, q, own, before)


STEP = 4
STEPS = TOPK // STEP
WIDE = STEP * BL
LOG2E = math.log2(math.e)


def attend_kernel(
    ids_ref, gate_ref, q_ref, mem_ref, local_ref, out_ref, kbuf, vbuf, s_scr, high, total, acc, sems
):
    rows_here = GROUP * QB
    keys = pltpu.make_async_copy(mem_ref.at[:, 0], kbuf, sems.at[0])
    values = pltpu.make_async_copy(mem_ref.at[:, 1], vbuf, sems.at[1])
    keys.start()
    values.start()
    high[...] = jnp.full_like(high, -jnp.inf)
    total[...] = jnp.zeros_like(total)
    acc[...] = jnp.zeros_like(acc)

    def some(block, i, buf):
        return jnp.concatenate(
            [buf[owner_of(ids_ref[block, 0, STEP * i + j])] for j in range(STEP)], axis=0
        )

    def fold(op, x):
        out = x[:, :HD]
        for j in range(1, STEP):
            out = op(out, x[:, j * HD : (j + 1) * HD])
        return out

    def score(block, i):
        q = q_ref[:, block * QB : (block + 1) * QB, :].reshape(rows_here, HD)
        sc = lax.dot_general(
            q, some(block, i, kbuf), (((1,), (1,)), ((), ())), preferred_element_type=jnp.float32
        )
        s_scr[block, i] = sc
        high[block] = jnp.maximum(high[block], fold(jnp.maximum, sc))

    factor = SCALE * LOG2E

    def settle(block):
        top = jnp.max(high[block], axis=1, keepdims=True) * factor
        high[block] = jnp.broadcast_to(top, (rows_here, HD))

    def weigh(block, i):
        top = high[block]
        w = [jnp.exp2(s_scr[block, i, :, j * HD : (j + 1) * HD] * factor - top) for j in range(STEP)]
        total[block] += (w[0] + w[1]) + (w[2] + w[3])
        w = jnp.concatenate([one.astype(jnp.bfloat16) for one in w], axis=1)
        acc[block] += jnp.dot(w, some(block, i, vbuf), preferred_element_type=jnp.float32)

    def finish(block):
        out = acc[block] / jnp.sum(total[block], axis=1, keepdims=True)
        for g in range(GROUP):
            rows = slice(g * QB, (g + 1) * QB)
            out_ref[pl.ds(block * QB, QB), pl.ds(g * HD, HD)] = (
                out[rows] * gate_ref[g] + local_ref[block, rows]
            ).astype(jnp.bfloat16)

    def first(i, carry):
        score(0, i)
        return carry

    def both(i, carry):
        weigh(0, i)
        score(1, i)
        return carry

    def last(i, carry):
        weigh(1, i)
        return carry

    keys.wait()
    lax.fori_loop(0, STEPS, first, 0, unroll=2)
    settle(0)
    values.wait()
    lax.fori_loop(0, STEPS, both, 0, unroll=2)
    settle(1)
    finish(0)
    lax.fori_loop(0, STEPS, last, 0, unroll=2)
    finish(1)


def attend(ids, gate, q, mem, local):
    rows = GROUP * QB
    return pl.pallas_call(
        attend_kernel,
        out_shape=jax.ShapeDtypeStruct((2 * QB, GROUP * HD), jnp.bfloat16),
        grid_spec=pltpu.PrefetchScalarGridSpec(
            num_scalar_prefetch=2,
            grid=(1,),
            in_specs=[
                whole_spec(q.shape),
                pl.BlockSpec(memory_space=pltpu.HBM),
                whole_spec(local.shape),
            ],
            out_specs=whole_spec((2 * QB, GROUP * HD)),
            scratch_shapes=[pltpu.VMEM((OWNERS, BL, HD), jnp.bfloat16)] * 2
            + [pltpu.VMEM((2, STEPS, rows, WIDE), jnp.float32)]
            + [pltpu.VMEM((2, rows, HD), jnp.float32)] * 3
            + [pltpu.SemaphoreType.DMA((2,))],
        ),
        compiler_params=pltpu.CompilerParams(vmem_limit_bytes=48 << 20),
        name="attend",
    )(ids, gate, q, mem, local)


def per_device(
    queries, local_keys, local_values, memory_keys, memory_values, block_ids, mixing_offset_per_head
):
    owners = lax.axis_size("mem")
    heads = lax.axis_size("head")
    here = memory_keys.shape[0] // BL
    mem_index = lax.axis_index("mem")
    head_index = lax.axis_index("head")

    wanted = lax.all_to_all(requests(block_ids), "mem", split_axis=0, concat_axis=0, tiled=True)
    blocks = gather_blocks(
        wanted, memory_keys.reshape(here, BL, HD), memory_values.reshape(here, BL, HD)
    )
    mem = lax.all_to_all(blocks, "mem", split_axis=0, concat_axis=0, tiled=True)

    rows = queries.shape[0]
    packed = jnp.concatenate(
        [
            queries.reshape(rows, heads, -1),
            local_keys.reshape(rows, heads, -1),
            local_values.reshape(rows, heads, -1),
        ],
        axis=2,
    ).transpose(1, 0, 2)
    parts = []
    for d in range(heads):
        mine = lax.dynamic_index_in_dim(packed, (head_index + d) % heads, 0, keepdims=False)
        if d:
            mine = lax.ppermute(mine, "head", [(i, (i + d) % heads) for i in range(heads)])
        parts.append(mine)
    place = jnp.stack([mem_index, head_index]).astype(jnp.int32)
    q, own = assemble(place, parts)
    before = lax.ppermute(own, "mem", [(i, i + 1) for i in range(owners - 1)])
    gate = jax.nn.sigmoid(mixing_offset_per_head)
    local = local_attention(place, gate, q, own, before)
    out = attend(block_ids, gate, q, mem, local)
    return lax.all_to_all(out, "head", split_axis=0, concat_axis=1, tiled=True)


def solution(mesh):
    return jax.shard_map(
        per_device,
        mesh=mesh,
        in_specs=(
            P(("mem", "head"), None),
            P(("mem", "head"), None),
            P(("mem", "head"), None),
            P("mem", "head"),
            P("mem", "head"),
            P("mem", "head", None),
            P("head"),
        ),
        out_specs=P(("mem", "head"), None),
        check_vma=False,
    )
```

```python
import functools
import math

import jax
import jax.numpy as jnp
from jax import lax
from jax.experimental import pallas as pl
from jax.experimental.pallas import tpu as pltpu
from jax.sharding import PartitionSpec as P

HD = 128
QB = 128
BL = 128
TOPK = 32
WINDOW = 256
GROUP = 4
OWNERS = 64
HERE = 32
SCALE = 1.0 / math.sqrt(HD)


def owner_of(block):
    return lax.shift_right_logical(block, 5)


def request_kernel(ids_ref, out_ref):
    out_ref[...] = jnp.zeros_like(out_ref)

    def ask(i, carry):
        for block in range(2):
            at = ids_ref[block, 0, i]
            out_ref[pl.ds(owner_of(at), 1), :] = jnp.full((1, 128), at & (HERE - 1), jnp.int32)
        return carry

    lax.fori_loop(0, TOPK, ask, 0, unroll=8)


def requests(ids):
    return pl.pallas_call(
        request_kernel,
        out_shape=jax.ShapeDtypeStruct((OWNERS, 128), jnp.int32),
        grid_spec=pltpu.PrefetchScalarGridSpec(
            num_scalar_prefetch=1,
            grid=(1,),
            in_specs=[],
            out_specs=pl.BlockSpec((OWNERS, 128), lambda i, *_: (0, 0)),
        ),
        compiler_params=pltpu.CompilerParams(vmem_limit_bytes=62 << 20),
        name="requests",
    )(ids)


PARTS = 4


def gather_kernel(idx_ref, keys_ref, values_ref, out_ref, kbuf, vbuf, picked, load_sem, store_sem):
    count = OWNERS // PARTS
    loads = []
    for part in range(2):
        rows = pl.ds(part * (HERE // 2), HERE // 2)
        loads.append(pltpu.make_async_copy(keys_ref.at[rows], kbuf.at[rows], load_sem.at[0, part]))
        loads.append(pltpu.make_async_copy(values_ref.at[rows], vbuf.at[rows], load_sem.at[1, part]))
    for load in loads:
        load.start()
    for load in loads:
        load.wait()
    stores = []
    for part in range(PARTS):
        for i in range(part * count, (part + 1) * count):
            at = idx_ref[i, 0]
            picked[i, 0] = kbuf[at]
            picked[i, 1] = vbuf[at]
        rows = pl.ds(part * count, count)
        stores.append(pltpu.make_async_copy(picked.at[rows], out_ref.at[rows], store_sem.at[part]))
        stores[-1].start()
    for store in stores:
        store.wait()


def gather_blocks(idx, keys, values):
    shape = (OWNERS, 2) + keys.shape[1:]
    hbm = pl.BlockSpec(memory_space=pltpu.HBM)
    return pl.pallas_call(
        gather_kernel,
        out_shape=jax.ShapeDtypeStruct(shape, keys.dtype),
        grid_spec=pltpu.PrefetchScalarGridSpec(
            num_scalar_prefetch=1,
            grid=(1,),
            in_specs=[hbm, hbm],
            out_specs=hbm,
            scratch_shapes=[pltpu.VMEM(keys.shape, keys.dtype)] * 2
            + [pltpu.VMEM(shape, keys.dtype)]
            + [pltpu.SemaphoreType.DMA((2, 2)), pltpu.SemaphoreType.DMA((PARTS,))],
        ),
        compiler_params=pltpu.CompilerParams(vmem_limit_bytes=62 << 20),
        name="gather_blocks",
    )(idx, keys, values)


def assemble_kernel(place_ref, *refs):
    parts, (q_ref, kv_ref) = refs[:8], refs[8:]
    for d in range(8):
        rows = pl.ds(pl.multiple_of(lax.rem(place_ref[1] + 8 - d, 8) * 32, 32), 32)
        for g in range(GROUP):
            q_ref[g, rows, :] = parts[d][:, pl.ds(g * HD, HD)]
        kv_ref[0, rows, :] = parts[d][:, pl.ds(4 * HD, HD)]
        kv_ref[1, rows, :] = parts[d][:, pl.ds(5 * HD, HD)]


def whole_spec(shape):
    return pl.BlockSpec(shape, lambda b, *_: (0,) * len(shape))


def assemble(place, parts):
    shapes = ((GROUP, 2 * QB, HD), (2, 2 * QB, HD))
    return pl.pallas_call(
        assemble_kernel,
        out_shape=tuple(jax.ShapeDtypeStruct(shape, jnp.bfloat16) for shape in shapes),
        grid_spec=pltpu.PrefetchScalarGridSpec(
            num_scalar_prefetch=1,
            grid=(1,),
            in_specs=[whole_spec(part.shape) for part in parts],
            out_specs=tuple(whole_spec(shape) for shape in shapes),
        ),
        compiler_params=pltpu.CompilerParams(vmem_limit_bytes=8 << 20),
        name="assemble",
    )(place, *parts)


def local_kernel(place_ref, gate_ref, q_ref, own_ref, before_ref, out_ref):
    block = pl.program_id(0)
    rows_here = GROUP * QB
    span = WINDOW + QB
    start = pl.multiple_of(block * QB, QB)
    q = q_ref[...].reshape(rows_here, HD)
    k = jnp.concatenate([before_ref[0], own_ref[0]], axis=0)
    v = jnp.concatenate([before_ref[1], own_ref[1]], axis=0)
    k = jnp.where(block == 0, k[:span], k[QB:])
    v = jnp.where(block == 0, v[:span], v[QB:])
    sc = lax.dot_general(q, k, (((1,), (1,)), ((), ())), preferred_element_type=jnp.float32) * SCALE
    t = lax.broadcasted_iota(jnp.int32, (QB, span), 0)
    s = lax.broadcasted_iota(jnp.int32, (QB, span), 1)
    apart = t + WINDOW - s
    known = place_ref[0] * (2 * QB) + start - WINDOW + s >= 0
    allowed = known & (apart >= 0) & (apart < WINDOW)
    sc = jnp.where(allowed[None], sc.reshape(GROUP, QB, span), -1e30).reshape(rows_here, span)
    w = jnp.exp(sc - jnp.max(sc, axis=1, keepdims=True))
    total = jnp.sum(w, axis=1, keepdims=True)
    out = jnp.dot(w.astype(jnp.bfloat16), v, preferred_element_type=jnp.float32) / total
    for g in range(GROUP):
        out_ref[0, pl.ds(g * QB, QB), :] = out[g * QB : (g + 1) * QB] * (1.0 - gate_ref[g])


def local_attention(place, gate, q, own, before):
    return pl.pallas_call(
        local_kernel,
        out_shape=jax.ShapeDtypeStruct((2, GROUP * QB, HD), jnp.float32),
        grid_spec=pltpu.PrefetchScalarGridSpec(
            num_scalar_prefetch=2,
            grid=(2,),
            in_specs=[
                pl.BlockSpec((GROUP, QB, HD), lambda b, *_: (0, b, 0)),
                whole_spec(own.shape),
                whole_spec(before.shape),
            ],
            out_specs=pl.BlockSpec((1, GROUP * QB, HD), lambda b, *_: (b, 0, 0)),
        ),
        compiler_params=pltpu.CompilerParams(vmem_limit_bytes=12 << 20),
        name="local",
    )(place, gate, q, own, before)


STEP = 4
STEPS = TOPK // STEP
WIDE = STEP * BL
LOG2E = math.log2(math.e)


def attend_kernel(
    ids_ref, gate_ref, q_ref, mem_ref, local_ref, out_ref, kbuf, vbuf, s_scr, high, total, acc, sems
):
    rows_here = GROUP * QB
    keys = pltpu.make_async_copy(mem_ref.at[:, 0], kbuf, sems.at[0])
    values = pltpu.make_async_copy(mem_ref.at[:, 1], vbuf, sems.at[1])
    keys.start()
    values.start()
    high[...] = jnp.full_like(high, -jnp.inf)
    total[...] = jnp.zeros_like(total)
    acc[...] = jnp.zeros_like(acc)

    def some(block, i, buf):
        return jnp.concatenate(
            [buf[owner_of(ids_ref[block, 0, STEP * i + j])] for j in range(STEP)], axis=0
        )

    def fold(op, x):
        out = x[:, :HD]
        for j in range(1, STEP):
            out = op(out, x[:, j * HD : (j + 1) * HD])
        return out

    def score(block, i):
        q = q_ref[:, block * QB : (block + 1) * QB, :].reshape(rows_here, HD)
        sc = lax.dot_general(
            q, some(block, i, kbuf), (((1,), (1,)), ((), ())), preferred_element_type=jnp.float32
        )
        s_scr[block, i] = sc
        high[block] = jnp.maximum(high[block], fold(jnp.maximum, sc))

    factor = SCALE * LOG2E

    def settle(block):
        top = jnp.max(high[block], axis=1, keepdims=True) * factor
        high[block] = jnp.broadcast_to(top, (rows_here, HD))

    def weigh(block, i):
        top = high[block]
        w = [jnp.exp2(s_scr[block, i, :, j * HD : (j + 1) * HD] * factor - top) for j in range(STEP)]
        total[block] += (w[0] + w[1]) + (w[2] + w[3])
        w = jnp.concatenate([one.astype(jnp.bfloat16) for one in w], axis=1)
        acc[block] += jnp.dot(w, some(block, i, vbuf), preferred_element_type=jnp.float32)

    def finish(block):
        out = acc[block] / jnp.sum(total[block], axis=1, keepdims=True)
        for g in range(GROUP):
            rows = slice(g * QB, (g + 1) * QB)
            out_ref[pl.ds(block * QB, QB), pl.ds(g * HD, HD)] = (
                out[rows] * gate_ref[g] + local_ref[block, rows]
            ).astype(jnp.bfloat16)

    def first(i, carry):
        score(0, i)
        return carry

    def both(i, carry):
        weigh(0, i)
        score(1, i)
        return carry

    def last(i, carry):
        weigh(1, i)
        return carry

    keys.wait()
    lax.fori_loop(0, STEPS, first, 0, unroll=4)
    settle(0)
    values.wait()
    lax.fori_loop(0, STEPS, both, 0, unroll=4)
    settle(1)
    finish(0)
    lax.fori_loop(0, STEPS, last, 0, unroll=4)
    finish(1)


def attend(ids, gate, q, mem, local):
    rows = GROUP * QB
    return pl.pallas_call(
        attend_kernel,
        out_shape=jax.ShapeDtypeStruct((2 * QB, GROUP * HD), jnp.bfloat16),
        grid_spec=pltpu.PrefetchScalarGridSpec(
            num_scalar_prefetch=2,
            grid=(1,),
            in_specs=[
                whole_spec(q.shape),
                pl.BlockSpec(memory_space=pltpu.HBM),
                whole_spec(local.shape),
            ],
            out_specs=whole_spec((2 * QB, GROUP * HD)),
            scratch_shapes=[pltpu.VMEM((OWNERS, BL, HD), jnp.bfloat16)] * 2
            + [pltpu.VMEM((2, STEPS, rows, WIDE), jnp.float32)]
            + [pltpu.VMEM((2, rows, HD), jnp.float32)] * 3
            + [pltpu.SemaphoreType.DMA((2,))],
        ),
        compiler_params=pltpu.CompilerParams(vmem_limit_bytes=48 << 20),
        name="attend",
    )(ids, gate, q, mem, local)


def per_device(
    queries, local_keys, local_values, memory_keys, memory_values, block_ids, mixing_offset_per_head
):
    owners = lax.axis_size("mem")
    heads = lax.axis_size("head")
    here = memory_keys.shape[0] // BL
    mem_index = lax.axis_index("mem")
    head_index = lax.axis_index("head")

    wanted = lax.all_to_all(requests(block_ids), "mem", split_axis=0, concat_axis=0, tiled=True)
    blocks = gather_blocks(
        wanted, memory_keys.reshape(here, BL, HD), memory_values.reshape(here, BL, HD)
    )
    mem = lax.all_to_all(blocks, "mem", split_axis=0, concat_axis=0, tiled=True)

    rows = queries.shape[0]
    packed = jnp.concatenate(
        [
            queries.reshape(rows, heads, -1),
            local_keys.reshape(rows, heads, -1),
            local_values.reshape(rows, heads, -1),
        ],
        axis=2,
    ).transpose(1, 0, 2)
    parts = []
    for d in range(heads):
        mine = lax.dynamic_index_in_dim(packed, (head_index + d) % heads, 0, keepdims=False)
        if d:
            mine = lax.ppermute(mine, "head", [(i, (i + d) % heads) for i in range(heads)])
        parts.append(mine)
    place = jnp.stack([mem_index, head_index]).astype(jnp.int32)
    q, own = assemble(place, parts)
    before = lax.ppermute(own, "mem", [(i, i + 1) for i in range(owners - 1)])
    gate = jax.nn.sigmoid(mixing_offset_per_head)
    local = local_attention(place, gate, q, own, before)
    out = attend(block_ids, gate, q, mem, local)
    return lax.all_to_all(out, "head", split_axis=0, concat_axis=1, tiled=True)


def solution(mesh):
    return jax.shard_map(
        per_device,
        mesh=mesh,
        in_specs=(
            P(("mem", "head"), None),
            P(("mem", "head"), None),
            P(("mem", "head"), None),
            P("mem", "head"),
            P("mem", "head"),
            P("mem", "head", None),
            P("head"),
        ),
        out_specs=P(("mem", "head"), None),
        check_vma=False,
    )
```

```python
import functools
import math

import jax
import jax.numpy as jnp
from jax import lax
from jax.experimental import pallas as pl
from jax.experimental.pallas import tpu as pltpu
from jax.sharding import PartitionSpec as P

HD = 128
QB = 128
BL = 128
TOPK = 32
WINDOW = 256
GROUP = 4
OWNERS = 64
HERE = 32
SCALE = 1.0 / math.sqrt(HD)


def owner_of(block):
    return lax.shift_right_logical(block, 5)


def request_kernel(ids_ref, out_ref):
    out_ref[...] = jnp.zeros_like(out_ref)

    def ask(i, carry):
        for block in range(2):
            at = ids_ref[block, 0, i]
            out_ref[pl.ds(owner_of(at), 1), :] = jnp.full((1, 128), at & (HERE - 1), jnp.int32)
        return carry

    lax.fori_loop(0, TOPK, ask, 0, unroll=8)


def requests(ids):
    return pl.pallas_call(
        request_kernel,
        out_shape=jax.ShapeDtypeStruct((OWNERS, 128), jnp.int32),
        grid_spec=pltpu.PrefetchScalarGridSpec(
            num_scalar_prefetch=1,
            grid=(1,),
            in_specs=[],
            out_specs=pl.BlockSpec((OWNERS, 128), lambda i, *_: (0, 0)),
        ),
        compiler_params=pltpu.CompilerParams(vmem_limit_bytes=4 << 20),
        name="requests",
    )(ids)


PARTS = 2


def gather_kernel(idx_ref, keys_ref, values_ref, out_ref, kbuf, vbuf, picked, load_sem, store_sem):
    count = OWNERS // PARTS
    sides = ((keys_ref, kbuf), (values_ref, vbuf))
    loads = [pltpu.make_async_copy(*pair, load_sem.at[side]) for side, pair in enumerate(sides)]
    for load in loads:
        load.start()
    stores = []
    for side, (_, buf) in enumerate(sides):
        loads[side].wait()
        for part in range(PARTS):
            for i in range(part * count, (part + 1) * count):
                picked[i, side] = buf[idx_ref[i, 0]]
            rows = pl.ds(part * count, count)
            stores.append(
                pltpu.make_async_copy(
                    picked.at[rows, side], out_ref.at[rows, side], store_sem.at[side, part]
                )
            )
            stores[-1].start()
    for store in stores:
        store.wait()


def gather_blocks(idx, keys, values):
    shape = (OWNERS, 2) + keys.shape[1:]
    hbm = pl.BlockSpec(memory_space=pltpu.HBM)
    return pl.pallas_call(
        gather_kernel,
        out_shape=jax.ShapeDtypeStruct(shape, keys.dtype),
        grid_spec=pltpu.PrefetchScalarGridSpec(
            num_scalar_prefetch=1,
            grid=(1,),
            in_specs=[hbm, hbm],
            out_specs=hbm,
            scratch_shapes=[pltpu.VMEM(keys.shape, keys.dtype)] * 2
            + [pltpu.VMEM(shape, keys.dtype)]
            + [pltpu.SemaphoreType.DMA((2,)), pltpu.SemaphoreType.DMA((2, PARTS))],
        ),
        compiler_params=pltpu.CompilerParams(vmem_limit_bytes=62 << 20),
        name="gather_blocks",
    )(idx, keys, values)


def assemble_kernel(place_ref, *refs):
    parts, (q_ref, kv_ref) = refs[:8], refs[8:]
    for d in range(8):
        rows = pl.ds(pl.multiple_of(lax.rem(place_ref[1] + 8 - d, 8) * 32, 32), 32)
        for g in range(GROUP):
            q_ref[g, rows, :] = parts[d][:, pl.ds(g * HD, HD)]
        kv_ref[0, rows, :] = parts[d][:, pl.ds(4 * HD, HD)]
        kv_ref[1, rows, :] = parts[d][:, pl.ds(5 * HD, HD)]


def whole_spec(shape):
    return pl.BlockSpec(shape, lambda b, *_: (0,) * len(shape))


def assemble(place, parts):
    shapes = ((GROUP, 2 * QB, HD), (2, 2 * QB, HD))
    return pl.pallas_call(
        assemble_kernel,
        out_shape=tuple(jax.ShapeDtypeStruct(shape, jnp.bfloat16) for shape in shapes),
        grid_spec=pltpu.PrefetchScalarGridSpec(
            num_scalar_prefetch=1,
            grid=(1,),
            in_specs=[whole_spec(part.shape) for part in parts],
            out_specs=tuple(whole_spec(shape) for shape in shapes),
        ),
        compiler_params=pltpu.CompilerParams(vmem_limit_bytes=8 << 20),
        name="assemble",
    )(place, *parts)


def local_kernel(place_ref, gate_ref, q_ref, own_ref, before_ref, out_ref):
    block = pl.program_id(0)
    rows_here = GROUP * QB
    span = WINDOW + QB
    start = pl.multiple_of(block * QB, QB)
    q = q_ref[...].reshape(rows_here, HD)
    k = jnp.concatenate([before_ref[0], own_ref[0]], axis=0)
    v = jnp.concatenate([before_ref[1], own_ref[1]], axis=0)
    k = jnp.where(block == 0, k[:span], k[QB:])
    v = jnp.where(block == 0, v[:span], v[QB:])
    sc = lax.dot_general(q, k, (((1,), (1,)), ((), ())), preferred_element_type=jnp.float32) * SCALE
    t = lax.broadcasted_iota(jnp.int32, (QB, span), 0)
    s = lax.broadcasted_iota(jnp.int32, (QB, span), 1)
    apart = t + WINDOW - s
    known = place_ref[0] * (2 * QB) + start - WINDOW + s >= 0
    allowed = known & (apart >= 0) & (apart < WINDOW)
    sc = jnp.where(allowed[None], sc.reshape(GROUP, QB, span), -1e30).reshape(rows_here, span)
    w = jnp.exp(sc - jnp.max(sc, axis=1, keepdims=True))
    total = jnp.sum(w, axis=1, keepdims=True)
    out = jnp.dot(w.astype(jnp.bfloat16), v, preferred_element_type=jnp.float32) / total
    for g in range(GROUP):
        out_ref[0, pl.ds(g * QB, QB), :] = out[g * QB : (g + 1) * QB] * (1.0 - gate_ref[g])


def local_attention(place, gate, q, own, before):
    return pl.pallas_call(
        local_kernel,
        out_shape=jax.ShapeDtypeStruct((2, GROUP * QB, HD), jnp.float32),
        grid_spec=pltpu.PrefetchScalarGridSpec(
            num_scalar_prefetch=2,
            grid=(2,),
            in_specs=[
                pl.BlockSpec((GROUP, QB, HD), lambda b, *_: (0, b, 0)),
                whole_spec(own.shape),
                whole_spec(before.shape),
            ],
            out_specs=pl.BlockSpec((1, GROUP * QB, HD), lambda b, *_: (b, 0, 0)),
        ),
        compiler_params=pltpu.CompilerParams(vmem_limit_bytes=12 << 20),
        name="local",
    )(place, gate, q, own, before)


STEP = 4
STEPS = TOPK // STEP
WIDE = STEP * BL
LOG2E = math.log2(math.e)


def attend_kernel(
    ids_ref, gate_ref, q_hbm, mem_ref, local_hbm, out_ref,
    q_ref, local_ref, kbuf, vbuf, s_scr, high, total, acc, sems,
):
    rows_here = GROUP * QB
    keys = pltpu.make_async_copy(mem_ref.at[:, 0], kbuf, sems.at[0])
    queries = pltpu.make_async_copy(q_hbm, q_ref, sems.at[1])
    values = pltpu.make_async_copy(mem_ref.at[:, 1], vbuf, sems.at[2])
    window = pltpu.make_async_copy(local_hbm, local_ref, sems.at[3])
    for copy in (keys, queries, values, window):
        copy.start()
    high[...] = jnp.full_like(high, -jnp.inf)
    total[...] = jnp.zeros_like(total)
    acc[...] = jnp.zeros_like(acc)

    def some(block, i, buf):
        return jnp.concatenate(
            [buf[owner_of(ids_ref[block, 0, STEP * i + j])] for j in range(STEP)], axis=0
        )

    def fold(op, x):
        out = x[:, :HD]
        for j in range(1, STEP):
            out = op(out, x[:, j * HD : (j + 1) * HD])
        return out

    def score(block, i):
        q = q_ref[:, block * QB : (block + 1) * QB, :].reshape(rows_here, HD)
        sc = lax.dot_general(
            q, some(block, i, kbuf), (((1,), (1,)), ((), ())), preferred_element_type=jnp.float32
        )
        s_scr[block, i] = sc
        high[block] = jnp.maximum(high[block], fold(jnp.maximum, sc))

    factor = SCALE * LOG2E

    def settle(block):
        top = jnp.max(high[block], axis=1, keepdims=True) * factor
        high[block] = jnp.broadcast_to(top, (rows_here, HD))

    def weigh(block, i):
        top = high[block]
        w = [jnp.exp2(s_scr[block, i, :, j * HD : (j + 1) * HD] * factor - top) for j in range(STEP)]
        total[block] += (w[0] + w[1]) + (w[2] + w[3])
        w = jnp.concatenate([one.astype(jnp.bfloat16) for one in w], axis=1)
        acc[block] += jnp.dot(w, some(block, i, vbuf), preferred_element_type=jnp.float32)

    def finish(block):
        out = acc[block] / jnp.sum(total[block], axis=1, keepdims=True)
        for g in range(GROUP):
            rows = slice(g * QB, (g + 1) * QB)
            out_ref[pl.ds(block * QB, QB), pl.ds(g * HD, HD)] = (
                out[rows] * gate_ref[g] + local_ref[block, rows]
            ).astype(jnp.bfloat16)

    def first(i, carry):
        score(0, i)
        return carry

    def both(i, carry):
        score(1, i)
        weigh(0, i)
        return carry

    def last(i, carry):
        weigh(1, i)
        return carry

    keys.wait()
    queries.wait()
    lax.fori_loop(0, STEPS, first, 0, unroll=8)
    settle(0)
    values.wait()
    lax.fori_loop(0, STEPS, both, 0, unroll=4)
    settle(1)
    window.wait()
    finish(0)
    lax.fori_loop(0, STEPS, last, 0, unroll=8)
    finish(1)


def attend(ids, gate, q, mem, local):
    rows = GROUP * QB
    return pl.pallas_call(
        attend_kernel,
        out_shape=jax.ShapeDtypeStruct((2 * QB, GROUP * HD), jnp.bfloat16),
        grid_spec=pltpu.PrefetchScalarGridSpec(
            num_scalar_prefetch=2,
            grid=(1,),
            in_specs=[pl.BlockSpec(memory_space=pltpu.HBM)] * 3,
            out_specs=whole_spec((2 * QB, GROUP * HD)),
            scratch_shapes=[pltpu.VMEM(q.shape, q.dtype), pltpu.VMEM(local.shape, local.dtype)]
            + [pltpu.VMEM((OWNERS, BL, HD), jnp.bfloat16)] * 2
            + [pltpu.VMEM((2, STEPS, rows, WIDE), jnp.float32)]
            + [pltpu.VMEM((2, rows, HD), jnp.float32)] * 3
            + [pltpu.SemaphoreType.DMA((4,))],
        ),
        compiler_params=pltpu.CompilerParams(vmem_limit_bytes=62 << 20),
        name="attend",
    )(ids, gate, q, mem, local)


def per_device(
    queries, local_keys, local_values, memory_keys, memory_values, block_ids, mixing_offset_per_head
):
    owners = lax.axis_size("mem")
    heads = lax.axis_size("head")
    here = memory_keys.shape[0] // BL
    mem_index = lax.axis_index("mem")
    head_index = lax.axis_index("head")

    wanted = lax.all_to_all(requests(block_ids), "mem", split_axis=0, concat_axis=0, tiled=True)
    blocks = gather_blocks(
        wanted, memory_keys.reshape(here, BL, HD), memory_values.reshape(here, BL, HD)
    )
    mem = lax.all_to_all(blocks, "mem", split_axis=0, concat_axis=0, tiled=True)

    rows = queries.shape[0]
    packed = jnp.concatenate(
        [
            queries.reshape(rows, heads, -1),
            local_keys.reshape(rows, heads, -1),
            local_values.reshape(rows, heads, -1),
        ],
        axis=2,
    ).transpose(1, 0, 2)
    parts = []
    for d in range(heads):
        mine = lax.dynamic_index_in_dim(packed, (head_index + d) % heads, 0, keepdims=False)
        if d:
            mine = lax.ppermute(mine, "head", [(i, (i + d) % heads) for i in range(heads)])
        parts.append(mine)
    place = jnp.stack([mem_index, head_index]).astype(jnp.int32)
    q, own = assemble(place, parts)
    before = lax.ppermute(own, "mem", [(i, i + 1) for i in range(owners - 1)])
    gate = jax.nn.sigmoid(mixing_offset_per_head)
    local = local_attention(place, gate, q, own, before)
    out = attend(block_ids, gate, q, mem, local)
    return lax.all_to_all(out, "head", split_axis=0, concat_axis=1, tiled=True)


def solution(mesh):
    return jax.shard_map(
        per_device,
        mesh=mesh,
        in_specs=(
            P(("mem", "head"), None),
            P(("mem", "head"), None),
            P(("mem", "head"), None),
            P("mem", "head"),
            P("mem", "head"),
            P("mem", "head", None),
            P("head"),
        ),
        out_specs=P(("mem", "head"), None),
        check_vma=False,
    )
```

```python
import functools
import math

import jax
import jax.numpy as jnp
from jax import lax
from jax.experimental import pallas as pl
from jax.experimental.pallas import tpu as pltpu
from jax.sharding import PartitionSpec as P

HD = 128
QB = 128
BL = 128
TOPK = 32
WINDOW = 256
GROUP = 4
OWNERS = 64
HERE = 32
SCALE = 1.0 / math.sqrt(HD)


def owner_of(block):
    return lax.shift_right_logical(block, 5)


def request_kernel(ids_ref, out_ref):
    out_ref[...] = jnp.zeros_like(out_ref)

    def ask(i, carry):
        for block in range(2):
            at = ids_ref[block, 0, i]
            out_ref[pl.ds(owner_of(at), 1), :] = jnp.full((1, 128), at & (HERE - 1), jnp.int32)
        return carry

    lax.fori_loop(0, TOPK, ask, 0, unroll=8)


def requests(ids):
    return pl.pallas_call(
        request_kernel,
        out_shape=jax.ShapeDtypeStruct((OWNERS, 128), jnp.int32),
        grid_spec=pltpu.PrefetchScalarGridSpec(
            num_scalar_prefetch=1,
            grid=(1,),
            in_specs=[],
            out_specs=pl.BlockSpec((OWNERS, 128), lambda i, *_: (0, 0)),
        ),
        compiler_params=pltpu.CompilerParams(vmem_limit_bytes=4 << 20),
        name="requests",
    )(ids)


PARTS = 2


def gather_kernel(idx_ref, keys_ref, values_ref, out_ref, kbuf, vbuf, picked, load_sem, store_sem):
    count = OWNERS // PARTS
    sides = ((keys_ref, kbuf), (values_ref, vbuf))
    loads = [pltpu.make_async_copy(*pair, load_sem.at[side]) for side, pair in enumerate(sides)]
    for load in loads:
        load.start()
    stores = []
    for side, (_, buf) in enumerate(sides):
        loads[side].wait()
        for part in range(PARTS):
            for i in range(part * count, (part + 1) * count):
                picked[i, side] = buf[idx_ref[i, 0]]
            rows = pl.ds(part * count, count)
            stores.append(
                pltpu.make_async_copy(
                    picked.at[rows, side], out_ref.at[rows, side], store_sem.at[side, part]
                )
            )
            stores[-1].start()
    for store in stores:
        store.wait()


def gather_blocks(idx, keys, values):
    shape = (OWNERS, 2) + keys.shape[1:]
    hbm = pl.BlockSpec(memory_space=pltpu.HBM)
    return pl.pallas_call(
        gather_kernel,
        out_shape=jax.ShapeDtypeStruct(shape, keys.dtype),
        grid_spec=pltpu.PrefetchScalarGridSpec(
            num_scalar_prefetch=1,
            grid=(1,),
            in_specs=[hbm, hbm],
            out_specs=hbm,
            scratch_shapes=[pltpu.VMEM(keys.shape, keys.dtype)] * 2
            + [pltpu.VMEM(shape, keys.dtype)]
            + [pltpu.SemaphoreType.DMA((2,)), pltpu.SemaphoreType.DMA((2, PARTS))],
        ),
        compiler_params=pltpu.CompilerParams(vmem_limit_bytes=62 << 20),
        name="gather_blocks",
    )(idx, keys, values)


def assemble_kernel(place_ref, *refs):
    parts, (q_ref, kv_ref) = refs[:8], refs[8:]
    for d in range(8):
        rows = pl.ds(pl.multiple_of(lax.rem(place_ref[1] + 8 - d, 8) * 32, 32), 32)
        for g in range(GROUP):
            q_ref[g, rows, :] = parts[d][:, pl.ds(g * HD, HD)]
        kv_ref[0, rows, :] = parts[d][:, pl.ds(4 * HD, HD)]
        kv_ref[1, rows, :] = parts[d][:, pl.ds(5 * HD, HD)]


def whole_spec(shape):
    return pl.BlockSpec(shape, lambda b, *_: (0,) * len(shape))


def assemble(place, parts):
    shapes = ((GROUP, 2 * QB, HD), (2, 2 * QB, HD))
    return pl.pallas_call(
        assemble_kernel,
        out_shape=tuple(jax.ShapeDtypeStruct(shape, jnp.bfloat16) for shape in shapes),
        grid_spec=pltpu.PrefetchScalarGridSpec(
            num_scalar_prefetch=1,
            grid=(1,),
            in_specs=[whole_spec(part.shape) for part in parts],
            out_specs=tuple(whole_spec(shape) for shape in shapes),
        ),
        compiler_params=pltpu.CompilerParams(vmem_limit_bytes=8 << 20),
        name="assemble",
    )(place, *parts)


def local_part(block, mem_index, q_ref, own_ref, before_ref):
    rows_here = GROUP * QB
    span = WINDOW + QB
    q = q_ref[:, block * QB : (block + 1) * QB, :].reshape(rows_here, HD)
    late = before_ref[:, block * QB :, :]
    early = own_ref[:, : (block + 1) * QB, :]
    k = jnp.concatenate([late[0], early[0]], axis=0)
    v = jnp.concatenate([late[1], early[1]], axis=0)
    sc = lax.dot_general(q, k, (((1,), (1,)), ((), ())), preferred_element_type=jnp.float32) * SCALE
    t = lax.broadcasted_iota(jnp.int32, (QB, span), 0)
    s = lax.broadcasted_iota(jnp.int32, (QB, span), 1)
    apart = t + WINDOW - s
    known = mem_index * (2 * QB) + block * QB - WINDOW + s >= 0
    allowed = known & (apart >= 0) & (apart < WINDOW)
    sc = jnp.where(allowed[None], sc.reshape(GROUP, QB, span), -1e30).reshape(rows_here, span)
    w = jnp.exp(sc - jnp.max(sc, axis=1, keepdims=True))
    total = jnp.sum(w, axis=1, keepdims=True)
    return jnp.dot(w.astype(jnp.bfloat16), v, preferred_element_type=jnp.float32) / total


STEP = 4
STEPS = TOPK // STEP
WIDE = STEP * BL
LOG2E = math.log2(math.e)


def attend_kernel(
    ids_ref, place_ref, gate_ref, q_ref, own_ref, before_ref, mem_ref, out_ref,
    local_ref, kbuf, vbuf, s_scr, high, total, acc, sems,
):
    rows_here = GROUP * QB
    keys = pltpu.make_async_copy(mem_ref.at[:, 0], kbuf, sems.at[0])
    values = pltpu.make_async_copy(mem_ref.at[:, 1], vbuf, sems.at[1])
    keys.start()
    values.start()
    for block in range(2):
        part = local_part(block, place_ref[0], q_ref, own_ref, before_ref)
        for g in range(GROUP):
            rows = slice(g * QB, (g + 1) * QB)
            local_ref[block, rows] = part[rows] * (1.0 - gate_ref[g])
    high[...] = jnp.full_like(high, -jnp.inf)
    total[...] = jnp.zeros_like(total)
    acc[...] = jnp.zeros_like(acc)

    def some(block, i, buf):
        return jnp.concatenate(
            [buf[owner_of(ids_ref[block, 0, STEP * i + j])] for j in range(STEP)], axis=0
        )

    def fold(op, x):
        out = x[:, :HD]
        for j in range(1, STEP):
            out = op(out, x[:, j * HD : (j + 1) * HD])
        return out

    def score(block, i):
        q = q_ref[:, block * QB : (block + 1) * QB, :].reshape(rows_here, HD)
        sc = lax.dot_general(
            q, some(block, i, kbuf), (((1,), (1,)), ((), ())), preferred_element_type=jnp.float32
        )
        s_scr[block, i] = sc
        high[block] = jnp.maximum(high[block], fold(jnp.maximum, sc))

    factor = SCALE * LOG2E

    def settle(block):
        top = jnp.max(high[block], axis=1, keepdims=True) * factor
        high[block] = jnp.broadcast_to(top, (rows_here, HD))

    def weigh(block, i):
        top = high[block]
        w = [jnp.exp2(s_scr[block, i, :, j * HD : (j + 1) * HD] * factor - top) for j in range(STEP)]
        total[block] += (w[0] + w[1]) + (w[2] + w[3])
        w = jnp.concatenate([one.astype(jnp.bfloat16) for one in w], axis=1)
        acc[block] += jnp.dot(w, some(block, i, vbuf), preferred_element_type=jnp.float32)

    def finish(block):
        out = acc[block] / jnp.sum(total[block], axis=1, keepdims=True)
        for g in range(GROUP):
            rows = slice(g * QB, (g + 1) * QB)
            out_ref[pl.ds(block * QB, QB), pl.ds(g * HD, HD)] = (
                out[rows] * gate_ref[g] + local_ref[block, rows]
            ).astype(jnp.bfloat16)

    def first(i, carry):
        score(0, i)
        return carry

    def both(i, carry):
        score(1, i)
        weigh(0, i)
        return carry

    def last(i, carry):
        weigh(1, i)
        return carry

    keys.wait()
    lax.fori_loop(0, STEPS, first, 0, unroll=8)
    settle(0)
    values.wait()
    lax.fori_loop(0, STEPS, both, 0, unroll=4)
    settle(1)
    finish(0)
    lax.fori_loop(0, STEPS, last, 0, unroll=8)
    finish(1)


def attend(ids, place, gate, q, own, before, mem):
    rows = GROUP * QB
    return pl.pallas_call(
        attend_kernel,
        out_shape=jax.ShapeDtypeStruct((2 * QB, GROUP * HD), jnp.bfloat16),
        grid_spec=pltpu.PrefetchScalarGridSpec(
            num_scalar_prefetch=3,
            grid=(1,),
            in_specs=[whole_spec(q.shape), whole_spec(own.shape), whole_spec(before.shape)]
            + [pl.BlockSpec(memory_space=pltpu.HBM)],
            out_specs=whole_spec((2 * QB, GROUP * HD)),
            scratch_shapes=[pltpu.VMEM((2, rows, HD), jnp.float32)]
            + [pltpu.VMEM((OWNERS, BL, HD), jnp.bfloat16)] * 2
            + [pltpu.VMEM((2, STEPS, rows, WIDE), jnp.float32)]
            + [pltpu.VMEM((2, rows, HD), jnp.float32)] * 3
            + [pltpu.SemaphoreType.DMA((2,))],
        ),
        compiler_params=pltpu.CompilerParams(vmem_limit_bytes=40 << 20),
        name="attend",
    )(ids, place, gate, q, own, before, mem)


def per_device(
    queries, local_keys, local_values, memory_keys, memory_values, block_ids, mixing_offset_per_head
):
    owners = lax.axis_size("mem")
    heads = lax.axis_size("head")
    here = memory_keys.shape[0] // BL
    mem_index = lax.axis_index("mem")
    head_index = lax.axis_index("head")

    wanted = lax.all_to_all(requests(block_ids), "mem", split_axis=0, concat_axis=0, tiled=True)
    blocks = gather_blocks(
        wanted, memory_keys.reshape(here, BL, HD), memory_values.reshape(here, BL, HD)
    )
    mem = lax.all_to_all(blocks, "mem", split_axis=0, concat_axis=0, tiled=True)

    rows = queries.shape[0]
    packed = jnp.concatenate(
        [
            queries.reshape(rows, heads, -1),
            local_keys.reshape(rows, heads, -1),
            local_values.reshape(rows, heads, -1),
        ],
        axis=2,
    ).transpose(1, 0, 2)
    parts = []
    for d in range(heads):
        mine = lax.dynamic_index_in_dim(packed, (head_index + d) % heads, 0, keepdims=False)
        if d:
            mine = lax.ppermute(mine, "head", [(i, (i + d) % heads) for i in range(heads)])
        parts.append(mine)
    place = jnp.stack([mem_index, head_index]).astype(jnp.int32)
    q, own = assemble(place, parts)
    before = lax.ppermute(own, "mem", [(i, i + 1) for i in range(owners - 1)])
    gate = jax.nn.sigmoid(mixing_offset_per_head)
    out = attend(block_ids, place, gate, q, own, before, mem)
    return lax.all_to_all(out, "head", split_axis=0, concat_axis=1, tiled=True)


def solution(mesh):
    return jax.shard_map(
        per_device,
        mesh=mesh,
        in_specs=(
            P(("mem", "head"), None),
            P(("mem", "head"), None),
            P(("mem", "head"), None),
            P("mem", "head"),
            P("mem", "head"),
            P("mem", "head", None),
            P("head"),
        ),
        out_specs=P(("mem", "head"), None),
        check_vma=False,
    )
```

```python
import functools
import math

import jax
import jax.numpy as jnp
from jax import lax
from jax.experimental import pallas as pl
from jax.experimental.pallas import tpu as pltpu
from jax.sharding import PartitionSpec as P

HD = 128
QB = 128
BL = 128
TOPK = 32
WINDOW = 256
GROUP = 4
OWNERS = 64
HERE = 32
SCALE = 1.0 / math.sqrt(HD)


def owner_of(block):
    return lax.shift_right_logical(block, 5)


def request_kernel(ids_ref, out_ref):
    owner = lax.broadcasted_iota(jnp.int32, (OWNERS, TOPK), 0)
    asked = jnp.zeros((OWNERS, TOPK), jnp.int32)
    for block in range(2):
        ids = jnp.broadcast_to(ids_ref[block], (OWNERS, TOPK))
        asked = jnp.maximum(asked, jnp.where(owner_of(ids) == owner, ids & (HERE - 1), 0))
    out_ref[...] = jnp.broadcast_to(jnp.max(asked, axis=1, keepdims=True), (OWNERS, 128))


def requests(ids):
    return pl.pallas_call(
        request_kernel,
        out_shape=jax.ShapeDtypeStruct((OWNERS, 128), jnp.int32),
        grid=(1,),
        in_specs=[pl.BlockSpec(ids.shape, lambda i: (0, 0, 0))],
        out_specs=pl.BlockSpec((OWNERS, 128), lambda i: (0, 0)),
        compiler_params=pltpu.CompilerParams(vmem_limit_bytes=62 << 20),
        name="requests",
    )(ids)


PARTS = 2


def gather_kernel(idx_ref, keys_ref, values_ref, out_ref, kbuf, vbuf, picked, load_sem, store_sem):
    count = OWNERS // PARTS
    sides = ((keys_ref, kbuf), (values_ref, vbuf))
    loads = [pltpu.make_async_copy(*pair, load_sem.at[side]) for side, pair in enumerate(sides)]
    for load in loads:
        load.start()
    stores = []
    for side, (_, buf) in enumerate(sides):
        loads[side].wait()
        for part in range(PARTS):
            for i in range(part * count, (part + 1) * count):
                picked[i, side] = buf[idx_ref[i, 0]]
            rows = pl.ds(part * count, count)
            stores.append(
                pltpu.make_async_copy(
                    picked.at[rows, side], out_ref.at[rows, side], store_sem.at[side, part]
                )
            )
            stores[-1].start()
    for store in stores:
        store.wait()


def gather_blocks(idx, keys, values):
    shape = (OWNERS, 2) + keys.shape[1:]
    hbm = pl.BlockSpec(memory_space=pltpu.HBM)
    return pl.pallas_call(
        gather_kernel,
        out_shape=jax.ShapeDtypeStruct(shape, keys.dtype),
        grid_spec=pltpu.PrefetchScalarGridSpec(
            num_scalar_prefetch=1,
            grid=(1,),
            in_specs=[hbm, hbm],
            out_specs=hbm,
            scratch_shapes=[pltpu.VMEM(keys.shape, keys.dtype)] * 2
            + [pltpu.VMEM(shape, keys.dtype)]
            + [pltpu.SemaphoreType.DMA((2,)), pltpu.SemaphoreType.DMA((2, PARTS))],
        ),
        compiler_params=pltpu.CompilerParams(vmem_limit_bytes=62 << 20),
        name="gather_blocks",
    )(idx, keys, values)


def assemble_kernel(place_ref, *refs):
    parts, (q_ref, kv_ref) = refs[:8], refs[8:]
    for d in range(8):
        rows = pl.ds(pl.multiple_of(lax.rem(place_ref[1] + 8 - d, 8) * 32, 32), 32)
        for g in range(GROUP):
            q_ref[g, rows, :] = parts[d][:, pl.ds(g * HD, HD)]
        kv_ref[0, rows, :] = parts[d][:, pl.ds(4 * HD, HD)]
        kv_ref[1, rows, :] = parts[d][:, pl.ds(5 * HD, HD)]


def whole_spec(shape):
    return pl.BlockSpec(shape, lambda b, *_: (0,) * len(shape))


def assemble(place, parts):
    shapes = ((GROUP, 2 * QB, HD), (2, 2 * QB, HD))
    return pl.pallas_call(
        assemble_kernel,
        out_shape=tuple(jax.ShapeDtypeStruct(shape, jnp.bfloat16) for shape in shapes),
        grid_spec=pltpu.PrefetchScalarGridSpec(
            num_scalar_prefetch=1,
            grid=(1,),
            in_specs=[whole_spec(part.shape) for part in parts],
            out_specs=tuple(whole_spec(shape) for shape in shapes),
        ),
        compiler_params=pltpu.CompilerParams(vmem_limit_bytes=8 << 20),
        name="assemble",
    )(place, *parts)


def local_part(block, mem_index, q_ref, own_ref, before_ref):
    rows_here = GROUP * QB
    span = WINDOW + QB
    q = q_ref[:, block * QB : (block + 1) * QB, :].reshape(rows_here, HD)
    late = before_ref[:, block * QB :, :]
    early = own_ref[:, : (block + 1) * QB, :]
    k = jnp.concatenate([late[0], early[0]], axis=0)
    v = jnp.concatenate([late[1], early[1]], axis=0)
    sc = lax.dot_general(q, k, (((1,), (1,)), ((), ())), preferred_element_type=jnp.float32) * SCALE
    t = lax.broadcasted_iota(jnp.int32, (QB, span), 0)
    s = lax.broadcasted_iota(jnp.int32, (QB, span), 1)
    apart = t + WINDOW - s
    known = mem_index * (2 * QB) + block * QB - WINDOW + s >= 0
    allowed = known & (apart >= 0) & (apart < WINDOW)
    sc = jnp.where(allowed[None], sc.reshape(GROUP, QB, span), -1e30).reshape(rows_here, span)
    w = jnp.exp(sc - jnp.max(sc, axis=1, keepdims=True))
    total = jnp.sum(w, axis=1, keepdims=True)
    return jnp.dot(w.astype(jnp.bfloat16), v, preferred_element_type=jnp.float32) / total


STEP = 4
STEPS = TOPK // STEP
WIDE = STEP * BL
LOG2E = math.log2(math.e)


def attend_kernel(
    ids_ref, place_ref, gate_ref, q_ref, own_ref, before_ref, mem_ref, out_ref,
    local_ref, kbuf, vbuf, s_scr, high, total, acc, sems,
):
    rows_here = GROUP * QB
    keys = pltpu.make_async_copy(mem_ref.at[:, 0], kbuf, sems.at[0])
    values = pltpu.make_async_copy(mem_ref.at[:, 1], vbuf, sems.at[1])
    keys.start()
    values.start()
    for block in range(2):
        part = local_part(block, place_ref[0], q_ref, own_ref, before_ref)
        for g in range(GROUP):
            rows = slice(g * QB, (g + 1) * QB)
            local_ref[block, rows] = part[rows] * (1.0 - gate_ref[g])
    high[...] = jnp.full_like(high, -jnp.inf)
    total[...] = jnp.zeros_like(total)
    acc[...] = jnp.zeros_like(acc)

    def some(block, i, buf):
        return jnp.concatenate(
            [buf[owner_of(ids_ref[block, 0, STEP * i + j])] for j in range(STEP)], axis=0
        )

    def fold(op, x):
        out = x[:, :HD]
        for j in range(1, STEP):
            out = op(out, x[:, j * HD : (j + 1) * HD])
        return out

    def score(block, i):
        q = q_ref[:, block * QB : (block + 1) * QB, :].reshape(rows_here, HD)
        sc = lax.dot_general(
            q, some(block, i, kbuf), (((1,), (1,)), ((), ())), preferred_element_type=jnp.float32
        )
        s_scr[block, i] = sc
        high[block] = jnp.maximum(high[block], fold(jnp.maximum, sc))

    factor = SCALE * LOG2E

    def settle(block):
        top = jnp.max(high[block], axis=1, keepdims=True) * factor
        high[block] = jnp.broadcast_to(top, (rows_here, HD))

    def weigh(block, i):
        top = high[block]
        w = [jnp.exp2(s_scr[block, i, :, j * HD : (j + 1) * HD] * factor - top) for j in range(STEP)]
        total[block] += (w[0] + w[1]) + (w[2] + w[3])
        w = jnp.concatenate([one.astype(jnp.bfloat16) for one in w], axis=1)
        acc[block] += jnp.dot(w, some(block, i, vbuf), preferred_element_type=jnp.float32)

    def finish(block):
        out = acc[block] / jnp.sum(total[block], axis=1, keepdims=True)
        for g in range(GROUP):
            rows = slice(g * QB, (g + 1) * QB)
            out_ref[pl.ds(block * QB, QB), pl.ds(g * HD, HD)] = (
                out[rows] * gate_ref[g] + local_ref[block, rows]
            ).astype(jnp.bfloat16)

    def scores(i, carry):
        score(0, i)
        score(1, i)
        return carry

    def weights(i, carry):
        weigh(0, i)
        weigh(1, i)
        return carry

    keys.wait()
    lax.fori_loop(0, STEPS, scores, 0, unroll=8)
    settle(0)
    settle(1)
    values.wait()
    lax.fori_loop(0, STEPS, weights, 0, unroll=4)
    finish(0)
    finish(1)


def attend(ids, place, gate, q, own, before, mem):
    rows = GROUP * QB
    return pl.pallas_call(
        attend_kernel,
        out_shape=jax.ShapeDtypeStruct((2 * QB, GROUP * HD), jnp.bfloat16),
        grid_spec=pltpu.PrefetchScalarGridSpec(
            num_scalar_prefetch=3,
            grid=(1,),
            in_specs=[whole_spec(q.shape), whole_spec(own.shape), whole_spec(before.shape)]
            + [pl.BlockSpec(memory_space=pltpu.HBM)],
            out_specs=whole_spec((2 * QB, GROUP * HD)),
            scratch_shapes=[pltpu.VMEM((2, rows, HD), jnp.float32)]
            + [pltpu.VMEM((OWNERS, BL, HD), jnp.bfloat16)] * 2
            + [pltpu.VMEM((2, STEPS, rows, WIDE), jnp.float32)]
            + [pltpu.VMEM((2, rows, HD), jnp.float32)] * 3
            + [pltpu.SemaphoreType.DMA((2,))],
        ),
        compiler_params=pltpu.CompilerParams(vmem_limit_bytes=40 << 20),
        name="attend",
    )(ids, place, gate, q, own, before, mem)


def per_device(
    queries, local_keys, local_values, memory_keys, memory_values, block_ids, mixing_offset_per_head
):
    owners = lax.axis_size("mem")
    heads = lax.axis_size("head")
    here = memory_keys.shape[0] // BL
    mem_index = lax.axis_index("mem")
    head_index = lax.axis_index("head")

    wanted = lax.all_to_all(requests(block_ids), "mem", split_axis=0, concat_axis=0, tiled=True)
    blocks = gather_blocks(
        wanted, memory_keys.reshape(here, BL, HD), memory_values.reshape(here, BL, HD)
    )
    mem = lax.all_to_all(blocks, "mem", split_axis=0, concat_axis=0, tiled=True)

    rows = queries.shape[0]
    packed = jnp.concatenate(
        [
            queries.reshape(rows, heads, -1),
            local_keys.reshape(rows, heads, -1),
            local_values.reshape(rows, heads, -1),
        ],
        axis=2,
    ).transpose(1, 0, 2)
    parts = []
    for d in range(heads):
        mine = lax.dynamic_index_in_dim(packed, (head_index + d) % heads, 0, keepdims=False)
        if d:
            mine = lax.ppermute(mine, "head", [(i, (i + d) % heads) for i in range(heads)])
        parts.append(mine)
    place = jnp.stack([mem_index, head_index]).astype(jnp.int32)
    q, own = assemble(place, parts)
    before = lax.ppermute(own, "mem", [(i, i + 1) for i in range(owners - 1)])
    gate = jax.nn.sigmoid(mixing_offset_per_head)
    out = attend(block_ids, place, gate, q, own, before, mem)
    return lax.all_to_all(out, "head", split_axis=0, concat_axis=1, tiled=True)


def solution(mesh):
    return jax.shard_map(
        per_device,
        mesh=mesh,
        in_specs=(
            P(("mem", "head"), None),
            P(("mem", "head"), None),
            P(("mem", "head"), None),
            P("mem", "head"),
            P("mem", "head"),
            P("mem", "head", None),
            P("head"),
        ),
        out_specs=P(("mem", "head"), None),
        check_vma=False,
    )
```

```python
import functools
import math

import jax
import jax.numpy as jnp
from jax import lax
from jax.experimental import pallas as pl
from jax.experimental.pallas import tpu as pltpu
from jax.sharding import PartitionSpec as P

HD = 128
QB = 128
BL = 128
TOPK = 32
WINDOW = 256
GROUP = 4
OWNERS = 64
HERE = 32
SCALE = 1.0 / math.sqrt(HD)


def owner_of(block):
    return lax.shift_right_logical(block, 5)


def request_kernel(ids_ref, out_ref):
    out_ref[...] = jnp.zeros_like(out_ref)

    def ask(i, carry):
        for block in range(2):
            at = ids_ref[block, 0, i]
            out_ref[pl.ds(owner_of(at), 1), :] = jnp.full((1, 128), at & (HERE - 1), jnp.int32)
        return carry

    lax.fori_loop(0, TOPK, ask, 0, unroll=8)


def requests(ids):
    return pl.pallas_call(
        request_kernel,
        out_shape=jax.ShapeDtypeStruct((OWNERS, 128), jnp.int32),
        grid_spec=pltpu.PrefetchScalarGridSpec(
            num_scalar_prefetch=1,
            grid=(1,),
            in_specs=[],
            out_specs=pl.BlockSpec((OWNERS, 128), lambda i, *_: (0, 0)),
        ),
        compiler_params=pltpu.CompilerParams(vmem_limit_bytes=4 << 20),
        name="requests",
    )(ids)


PARTS = 2


def gather_kernel(idx_ref, keys_ref, values_ref, out_ref, kbuf, vbuf, picked, load_sem, store_sem):
    count = OWNERS // PARTS
    sides = ((keys_ref, kbuf), (values_ref, vbuf))
    loads = [pltpu.make_async_copy(*pair, load_sem.at[side]) for side, pair in enumerate(sides)]
    for load in loads:
        load.start()
    stores = []
    for side, (_, buf) in enumerate(sides):
        loads[side].wait()
        for part in range(PARTS):
            for i in range(part * count, (part + 1) * count):
                picked[i, side] = buf[idx_ref[i, 0]]
            rows = pl.ds(part * count, count)
            stores.append(
                pltpu.make_async_copy(
                    picked.at[rows, side], out_ref.at[rows, side], store_sem.at[side, part]
                )
            )
            stores[-1].start()
    for store in stores:
        store.wait()


def gather_blocks(idx, keys, values):
    shape = (OWNERS, 2) + keys.shape[1:]
    hbm = pl.BlockSpec(memory_space=pltpu.HBM)
    return pl.pallas_call(
        gather_kernel,
        out_shape=jax.ShapeDtypeStruct(shape, keys.dtype),
        grid_spec=pltpu.PrefetchScalarGridSpec(
            num_scalar_prefetch=1,
            grid=(1,),
            in_specs=[hbm, hbm],
            out_specs=hbm,
            scratch_shapes=[pltpu.VMEM(keys.shape, keys.dtype)] * 2
            + [pltpu.VMEM(shape, keys.dtype)]
            + [pltpu.SemaphoreType.DMA((2,)), pltpu.SemaphoreType.DMA((2, PARTS))],
        ),
        compiler_params=pltpu.CompilerParams(vmem_limit_bytes=62 << 20),
        name="gather_blocks",
    )(idx, keys, values)


def assemble_kernel(place_ref, *refs):
    parts, (q_ref, kv_ref) = refs[:8], refs[8:]
    for d in range(8):
        rows = pl.ds(pl.multiple_of(lax.rem(place_ref[1] + 8 - d, 8) * 32, 32), 32)
        for g in range(GROUP):
            q_ref[g, rows, :] = parts[d][:, pl.ds(g * HD, HD)]
        kv_ref[0, rows, :] = parts[d][:, pl.ds(4 * HD, HD)]
        kv_ref[1, rows, :] = parts[d][:, pl.ds(5 * HD, HD)]


def whole_spec(shape):
    return pl.BlockSpec(shape, lambda b, *_: (0,) * len(shape))


def assemble(place, parts):
    shapes = ((GROUP, 2 * QB, HD), (2, 2 * QB, HD))
    return pl.pallas_call(
        assemble_kernel,
        out_shape=tuple(jax.ShapeDtypeStruct(shape, jnp.bfloat16) for shape in shapes),
        grid_spec=pltpu.PrefetchScalarGridSpec(
            num_scalar_prefetch=1,
            grid=(1,),
            in_specs=[whole_spec(part.shape) for part in parts],
            out_specs=tuple(whole_spec(shape) for shape in shapes),
        ),
        compiler_params=pltpu.CompilerParams(vmem_limit_bytes=8 << 20),
        name="assemble",
    )(place, *parts)


def local_part(block, mem_index, q_ref, own_ref, before_ref):
    rows_here = GROUP * QB
    span = WINDOW + QB
    q = q_ref[:, block * QB : (block + 1) * QB, :].reshape(rows_here, HD)
    late = before_ref[:, block * QB :, :]
    early = own_ref[:, : (block + 1) * QB, :]
    k = jnp.concatenate([late[0], early[0]], axis=0)
    v = jnp.concatenate([late[1], early[1]], axis=0)
    sc = lax.dot_general(q, k, (((1,), (1,)), ((), ())), preferred_element_type=jnp.float32) * SCALE
    t = lax.broadcasted_iota(jnp.int32, (QB, span), 0)
    s = lax.broadcasted_iota(jnp.int32, (QB, span), 1)
    apart = t + WINDOW - s
    known = mem_index * (2 * QB) + block * QB - WINDOW + s >= 0
    allowed = known & (apart >= 0) & (apart < WINDOW)
    sc = jnp.where(allowed[None], sc.reshape(GROUP, QB, span), -1e30).reshape(rows_here, span)
    w = jnp.exp(sc - jnp.max(sc, axis=1, keepdims=True))
    total = jnp.sum(w, axis=1, keepdims=True)
    return jnp.dot(w.astype(jnp.bfloat16), v, preferred_element_type=jnp.float32) / total


STEP = 4
STEPS = TOPK // STEP
WIDE = STEP * BL
LOG2E = math.log2(math.e)


def attend_kernel(
    ids_ref, place_ref, gate_ref, q_ref, own_ref, before_ref, mem_ref, out_ref,
    local_ref, kbuf, vbuf, s_scr, high, total, acc, sems,
):
    rows_here = GROUP * QB
    keys = pltpu.make_async_copy(mem_ref.at[:, 0], kbuf, sems.at[0])
    values = pltpu.make_async_copy(mem_ref.at[:, 1], vbuf, sems.at[1])
    keys.start()
    values.start()
    for block in range(2):
        part = local_part(block, place_ref[0], q_ref, own_ref, before_ref)
        for g in range(GROUP):
            rows = slice(g * QB, (g + 1) * QB)
            local_ref[block, rows] = part[rows] * (1.0 - gate_ref[g])
    high[...] = jnp.full_like(high, -jnp.inf)
    total[...] = jnp.zeros_like(total)
    acc[...] = jnp.zeros_like(acc)

    def some(block, i, buf):
        return jnp.concatenate(
            [buf[owner_of(ids_ref[block, 0, STEP * i + j])] for j in range(STEP)], axis=0
        )

    def fold(op, x):
        out = x[:, :HD]
        for j in range(1, STEP):
            out = op(out, x[:, j * HD : (j + 1) * HD])
        return out

    def score(block, i):
        q = q_ref[:, block * QB : (block + 1) * QB, :].reshape(rows_here, HD)
        sc = lax.dot_general(
            q, some(block, i, kbuf), (((1,), (1,)), ((), ())), preferred_element_type=jnp.float32
        )
        s_scr[block, i] = sc
        high[block] = jnp.maximum(high[block], fold(jnp.maximum, sc))

    factor = SCALE * LOG2E

    def settle(block):
        top = jnp.max(high[block], axis=1, keepdims=True) * factor
        high[block] = jnp.broadcast_to(top, (rows_here, HD))

    def weigh(block, i):
        top = high[block]
        w = [jnp.exp2(s_scr[block, i, :, j * HD : (j + 1) * HD] * factor - top) for j in range(STEP)]
        total[block] += (w[0] + w[1]) + (w[2] + w[3])
        w = jnp.concatenate([one.astype(jnp.bfloat16) for one in w], axis=1)
        acc[block] += jnp.dot(w, some(block, i, vbuf), preferred_element_type=jnp.float32)

    def finish(block):
        out = acc[block] / jnp.sum(total[block], axis=1, keepdims=True)
        for g in range(GROUP):
            rows = slice(g * QB, (g + 1) * QB)
            out_ref[pl.ds(block * QB, QB), pl.ds(g * HD, HD)] = (
                out[rows] * gate_ref[g] + local_ref[block, rows]
            ).astype(jnp.bfloat16)

    def scores(i, carry):
        score(0, i)
        score(1, i)
        return carry

    def weights(i, carry):
        weigh(0, i)
        weigh(1, i)
        return carry

    keys.wait()
    lax.fori_loop(0, STEPS, scores, 0, unroll=8)
    settle(0)
    settle(1)
    values.wait()
    lax.fori_loop(0, STEPS, weights, 0, unroll=4)
    finish(0)
    finish(1)


def attend(ids, place, gate, q, own, before, mem):
    rows = GROUP * QB
    return pl.pallas_call(
        attend_kernel,
        out_shape=jax.ShapeDtypeStruct((2 * QB, GROUP * HD), jnp.bfloat16),
        grid_spec=pltpu.PrefetchScalarGridSpec(
            num_scalar_prefetch=3,
            grid=(1,),
            in_specs=[whole_spec(q.shape), whole_spec(own.shape), whole_spec(before.shape)]
            + [pl.BlockSpec(memory_space=pltpu.HBM)],
            out_specs=whole_spec((2 * QB, GROUP * HD)),
            scratch_shapes=[pltpu.VMEM((2, rows, HD), jnp.float32)]
            + [pltpu.VMEM((OWNERS, BL, HD), jnp.bfloat16)] * 2
            + [pltpu.VMEM((2, STEPS, rows, WIDE), jnp.float32)]
            + [pltpu.VMEM((2, rows, HD), jnp.float32)] * 3
            + [pltpu.SemaphoreType.DMA((2,))],
        ),
        compiler_params=pltpu.CompilerParams(vmem_limit_bytes=40 << 20),
        name="attend",
    )(ids, place, gate, q, own, before, mem)


def per_device(
    queries, local_keys, local_values, memory_keys, memory_values, block_ids, mixing_offset_per_head
):
    owners = lax.axis_size("mem")
    heads = lax.axis_size("head")
    here = memory_keys.shape[0] // BL
    mem_index = lax.axis_index("mem")
    head_index = lax.axis_index("head")

    wanted = lax.all_to_all(requests(block_ids), "mem", split_axis=0, concat_axis=0, tiled=True)
    blocks = gather_blocks(
        wanted, memory_keys.reshape(here, BL, HD), memory_values.reshape(here, BL, HD)
    )
    mem = lax.all_to_all(blocks, "mem", split_axis=0, concat_axis=0, tiled=True)

    rows = queries.shape[0]
    packed = jnp.concatenate(
        [
            queries.reshape(rows, heads, -1),
            local_keys.reshape(rows, heads, -1),
            local_values.reshape(rows, heads, -1),
        ],
        axis=2,
    ).transpose(1, 0, 2)
    parts = []
    for d in range(heads):
        mine = lax.dynamic_index_in_dim(packed, (head_index + d) % heads, 0, keepdims=False)
        if d:
            mine = lax.ppermute(mine, "head", [(i, (i + d) % heads) for i in range(heads)])
        parts.append(mine)
    place = jnp.stack([mem_index, head_index]).astype(jnp.int32)
    q, own = assemble(place, parts)
    before = lax.ppermute(own, "mem", [(i, i + 1) for i in range(owners - 1)])
    gate = jax.nn.sigmoid(mixing_offset_per_head)
    out = attend(block_ids, place, gate, q, own, before, mem)
    return lax.all_to_all(out, "head", split_axis=0, concat_axis=1, tiled=True)


def solution(mesh):
    return jax.shard_map(
        per_device,
        mesh=mesh,
        in_specs=(
            P(("mem", "head"), None),
            P(("mem", "head"), None),
            P(("mem", "head"), None),
            P("mem", "head"),
            P("mem", "head"),
            P("mem", "head", None),
            P("head"),
        ),
        out_specs=P(("mem", "head"), None),
        check_vma=False,
    )
```
